512 devices in a mesh: row: 16 (over z_lo, core), col: 4 (over x), layer: 8 (over y, z_hi).
Axes of the slice: x: 4, y: 4, z: 16 (z_hi: 2, z_lo: 8; z = z_hi * 8 + z_lo), core: 2. Of those that a mesh axis runs over, the one named last changes fastest.
Arguments:
- density: bfloat16 [1024, 11, 128, 128], P(('row', 'layer'), None, 'col'), may hold values from -1.5 to 1.5, as said below
- pattern: int32 [1024, 11], replicated, may hold values from -1 to 1023, as said below
- square_filter: int32 [1024, 12], replicated, may hold values from 0 to 1023, as said below
- cube_filter: int32 [1024, 16], replicated, may hold values from 0 to 1023, as said below
Outputs:
- purified: float32 [1024, 16, 128, 128], P(('row', 'layer'), 'col')
The draws below stay inside these ranges and needn't reach their ends.
Inputs may be any that keep to these rules, and one draw needn't show every extreme that they name: `density`: slot s of block row i holds the block of P at (i, pattern[i, s]), and zeros where pattern[i, s] is -1; the matrix so described is exactly symmetric. Row i lists distinct block columns, each within 5 of i modulo 1024, i itself among them; unused slots hold -1; the block pattern is symmetric; some block row uses all 11 slots. `square_filter`: row i lists 12 distinct block columns, each within 10 of i modulo 1024. `cube_filter`: row i lists 16 distinct block columns, each within 15 of i modulo 1024.
All inputs are finite; a program needn't handle non-finite values.
Results may differ from the reference program's by a relative error of at most 0.0023.
Values may be sent and summed in bfloat16 or wider, within the bound.
A program may use at most 64 MiB of HBM per device.

```python
import jax
import jax.numpy as jnp
from jax import lax

BLOCK = 128
RADIUS = 5
SLOTS = 11
SQ_SLOTS = 12
CUBE_SLOTS = 16
NB = 1024


def live_band(key):
    coins = jax.random.randint(jax.random.fold_in(key, 41), (NB, RADIUS), 0, 10) < 7
    full_row = jax.random.randint(jax.random.fold_in(key, 42), (), 0, NB)
    rows = jnp.arange(NB)
    steps = jnp.arange(1, RADIUS + 1)
    edges = coins | (rows[:, None] == full_row) | (rows[:, None] == (full_row - steps[None, :]) % NB)
    offsets = jnp.arange(SLOTS) - RADIUS
    base = jnp.where(offsets[None, :] > 0, rows[:, None], (rows[:, None] + offsets[None, :]) % NB)
    gap = jnp.clip(jnp.abs(offsets) - 1, 0, RADIUS - 1)
    live = jnp.where(offsets[None, :] == 0, True, edges[base, gap[None, :]])
    ranks = jnp.where(live, 0, SLOTS) + jnp.arange(SLOTS)[None, :]
    order = jnp.argsort(ranks, axis=1, stable=True)
    return (live, base, gap, offsets, order)


def draw_pattern(key, part):
    live, base, gap, offsets, order = live_band(jax.random.fold_in(key, 40))
    rows = jnp.arange(NB)
    columns = jnp.where(live, (rows[:, None] + offsets[None, :]) % NB, -1)
    return jnp.take_along_axis(columns, order, axis=1).astype(jnp.int32)


def draw_density(key, part):
    live, base, gap, offsets, order = live_band(jax.random.fold_in(key, 40))
    noise_key = jax.random.fold_in(key, 51)
    diag_key = jax.random.fold_in(key, 52)
    pair_noise = 0.08 * jnp.clip(jax.random.normal(noise_key, (NB, RADIUS, BLOCK, BLOCK), jnp.float32), -4.0, 4.0)
    diag_noise = 0.08 * jnp.clip(jax.random.normal(diag_key, (NB, BLOCK, BLOCK), jnp.float32), -4.0, 4.0)
    identity = (jnp.arange(BLOCK)[:, None] == jnp.arange(BLOCK)[None, :]).astype(jnp.float32)
    diag_block = 0.5 * identity[None] + 0.7071 * (diag_noise + jnp.swapaxes(diag_noise, 1, 2))
    picked = pair_noise[base, gap[None, :]]
    flipped = jnp.swapaxes(picked, 2, 3)
    band = jnp.where(offsets[None, :, None, None] < 0, flipped, picked)
    band = jnp.where(offsets[None, :, None, None] == 0, diag_block[:, None], band)
    band = band * live[:, :, None, None].astype(jnp.float32)
    return jnp.take_along_axis(band, order[:, :, None, None], axis=1).astype(jnp.bfloat16)


def window_filter(key, reach, keep):
    width = 2 * reach + 1
    scores = jax.random.randint(key, (NB, width), 0, 1 << 20) * width + jnp.arange(width)[None, :]
    chosen = jnp.argsort(scores, axis=1, stable=True)[:, :keep]
    return ((jnp.arange(NB)[:, None] + chosen - reach) % NB).astype(jnp.int32)


def draw_square_filter(key, part):
    return window_filter(jax.random.fold_in(key, 61), 2 * RADIUS, SQ_SLOTS)


def draw_cube_filter(key, part):
    return window_filter(jax.random.fold_in(key, 71), 3 * RADIUS, CUBE_SLOTS)


def setup_inputs(seed: int = 0) -> dict:
    arg_keys = jax.random.split(jax.random.key(seed), 5)
    return {
        "density": draw_density(jax.random.fold_in(arg_keys[4], 71), 0),
        "pattern": draw_pattern(jax.random.fold_in(arg_keys[4], 71), 0),
        "square_filter": draw_square_filter(jax.random.fold_in(arg_keys[4], 71), 0),
        "cube_filter": draw_cube_filter(jax.random.fold_in(arg_keys[4], 71), 0),
    }


def matched_slots(listed, targets):
    match = listed[:, None, :] == targets[None, :, None]
    slot_ids = jnp.arange(listed.shape[1], dtype=jnp.int32)
    picked_slot = jnp.sum(jnp.where(match, slot_ids[None, None, :], 0), axis=2).astype(jnp.int32)
    return picked_slot, jnp.any(match, axis=2)


def product_row(row, left_blocks, right_blocks, right_lists, pattern, targets):
    listed = pattern[row]
    source = jnp.where(listed >= 0, listed, row).astype(jnp.int32)
    right_listed = right_lists[source]
    picked_slot, found = matched_slots(right_listed, targets)
    picked = right_blocks[source[:, None], picked_slot]
    picked = jnp.where(found[:, :, None, None], picked, jnp.zeros((), picked.dtype))
    left = left_blocks[row].astype(jnp.float32)
    return jnp.einsum("axy,ajyz->jxz", left, picked.astype(jnp.float32))


def reference(density, pattern, square_filter, cube_filter):
    rows = jnp.arange(NB, dtype=jnp.int32)

    def square_row(row):
        return product_row(row, density, density, pattern, pattern, square_filter[row]).astype(jnp.bfloat16)

    square = lax.map(square_row, rows)

    def purified_row(row):
        targets = cube_filter[row]
        cube = product_row(row, density, square, square_filter, pattern, targets)
        chooser = (targets[:, None] == square_filter[row][None, :]).astype(jnp.float32)
        own_square = jnp.einsum("tj,jxz->txz", chooser, square[row].astype(jnp.float32))
        return 3.0 * own_square - 2.0 * cube

    return lax.map(purified_row, rows)
```

```python
import functools

import jax
import jax.numpy as jnp
from jax import lax
from jax.experimental import pallas as pl
from jax.experimental.pallas import tpu as pltpu
from jax.sharding import PartitionSpec as P

MESH = pl.DeviceIdType.MESH
RADIUS = 5
HALF = RADIUS + 1
BAND = 2 * RADIUS + 1
SQUARE_REACH = 2 * RADIUS
ROWS = 8
COLS = 4
BEFORE = 16
HELD = BEFORE + ROWS + 10
Z_CHUNKS = 2


def band_kernel(total_rows, first_row, pattern_ref, density_ref, upper_ref):
    upper_ref[...] = jnp.zeros_like(upper_ref)
    first = first_row[0]

    def row(i, carry):
        for s in range(density_ref.shape[1]):
            column = pattern_ref[i, s]
            offset = lax.rem(column - (first + i) + total_rows, total_rows)

            @pl.when((column >= 0) & (offset <= RADIUS))
            def _():
                upper_ref[i, offset] = density_ref[i, s]

        return carry

    lax.fori_loop(0, ROWS, row, 0)


def gather_kernel(upper_ref, held_ref, send, recv, local):
    row, col, layer = (lax.axis_index(a) for a in ("row", "col", "layer"))
    n_row, n_layer = lax.axis_size("row"), lax.axis_size("layer")
    side = lax.rem(layer, 2)
    up = lax.div(layer + 2, n_layer)
    down = 1 - lax.div(layer + n_layer - 2, n_layer)
    partner = {"layer": layer + 1 - 2 * side}
    after = {"row": lax.rem(row + up, n_row), "layer": lax.rem(layer + 2, n_layer)}
    before = {
        "row": lax.rem(row + n_row - down, n_row),
        "layer": lax.rem(layer + n_layer - 2, n_layer),
    }
    relay = {k: after[k] * (1 - side) + before[k] * side for k in after}
    right, left = lax.rem(col + 1, COLS), lax.rem(col + COLS - 1, COLS)

    barrier = pltpu.get_barrier_semaphore()
    for peer in (partner, after, before, {"col": left}, {"col": right}):
        pl.semaphore_signal(barrier, inc=1, device_id=peer, device_id_type=MESH)
    pl.semaphore_wait(barrier, 5)

    started = []

    def copy(src, dst, device):
        n = len(started)
        c = pltpu.make_async_remote_copy(
            src_ref=src,
            dst_ref=dst,
            send_sem=send.at[n],
            recv_sem=recv.at[n],
            device_id=device,
            device_id_type=MESH,
        )
        c.start()
        started.append(c)
        return c

    def spread(src, rows):
        return (
            copy(src, held_ref.at[col, rows], {"col": right}),
            copy(src, held_ref.at[col, rows], {"col": left}),
        )

    def forward(pair, rows):
        from_left, from_right = pair
        from_left.wait_recv()
        a = held_ref.at[left, rows, 0:3]
        to_right = copy(a, a, {"col": right})
        from_right.wait_recv()
        b = held_ref.at[right, rows, 3:HALF]
        to_left = copy(b, b, {"col": left})
        return to_right, to_left

    own = pl.ds(BEFORE, ROWS)
    keep = pltpu.make_async_copy(upper_ref, held_ref.at[col, own], local)
    keep.start()

    step = ROWS // Z_CHUNKS
    seen_as = 8 + 16 * side
    seen = 24 - 16 * side
    across = [
        copy(
            upper_ref.at[pl.ds(k * step, step)],
            held_ref.at[col, pl.ds(seen_as + k * step, step)],
            partner,
        )
        for k in range(Z_CHUNKS)
    ]
    own_pair = spread(upper_ref, own)
    far = pl.ds(1, ROWS - 1)
    far_copy = copy(upper_ref.at[far], held_ref.at[col, far], after)
    edge = pl.ds(BEFORE + 2 * ROWS, 2)
    edge_copy = copy(upper_ref.at[pl.ds(0, 2)], held_ref.at[col, edge], before)

    pending = []
    far_copy.wait_recv()
    far_pair = spread(held_ref.at[col, far], far)
    edge_copy.wait_recv()
    edge_pair = spread(held_ref.at[col, edge], edge)
    pending += forward(own_pair, own)
    relayed, pairs = [], []
    for k in range(Z_CHUNKS):
        across[k].wait_recv()
        got = pl.ds(seen + k * step, step)
        src = held_ref.at[col, got]
        put = pl.ds(seen_as + k * step, step)
        relayed.append((copy(src, held_ref.at[col, put], relay), put))
        pairs.append((spread(src, got), got))
    pending += forward(far_pair, far)
    pending += forward(edge_pair, edge)
    for c, rows in relayed:
        c.wait_recv()
        pairs.append((spread(held_ref.at[col, rows], rows), rows))
    for pair, rows in pairs:
        pending += forward(pair, rows)
    for c in pending:
        c.wait_recv()
    for c in started:
        c.wait_send()
    keep.wait()


N_COPIES = 2 + Z_CHUNKS * 2 + 4 * (3 + 2 * Z_CHUNKS)
BAND_ROWS = 39
SQUARE_ROWS = ROWS + 2 * RADIUS
SQUARE_COLUMNS = BAND_ROWS - 1


def product_kernel(
    total_rows, block, first_row, square_lists, targets, held_ref, out_ref, band, square, member, need
):
    first = first_row[0]
    offsets = 2 * SQUARE_REACH + 1

    def clear(k, carry):
        for e in range(offsets):
            member[k, e] = 0
            need[k, e] = 0
        return carry

    lax.fori_loop(0, SQUARE_ROWS, clear, 0)

    def listed(k, carry):
        for s in range(square_lists.shape[1]):
            e = lax.rem(
                square_lists[k, s] - (first + k - RADIUS) + SQUARE_REACH + 2 * total_rows,
                total_rows,
            )
            member[k, e] = 1
        return carry

    lax.fori_loop(0, SQUARE_ROWS, listed, 0)

    def place_of(i, t):
        return lax.rem(
            targets[i, t] - first + 3 * RADIUS + 2 * total_rows, total_rows
        )

    def wanted(i, carry):
        for t in range(targets.shape[1]):
            place = place_of(i, t)
            for q in range(BAND):
                k = i + q
                e = place - 3 * RADIUS - (k - RADIUS) + SQUARE_REACH
                inside = (e >= 0) & (e < offsets)
                hit = inside & (member[k, jnp.clip(e, 0, offsets - 1)] == 1)

                @pl.when(hit)
                def _():
                    need[k, e] = 1

                @pl.when(jnp.logical_not(hit))
                def _():
                    square[place, pl.ds(pl.multiple_of(k * block, block), block), :] = (
                        jnp.zeros((block, block), square.dtype)
                    )

        return carry

    lax.fori_loop(0, ROWS, wanted, 0)

    def unfold(a, carry):
        for d in range(HALF):
            whole = jnp.concatenate([held_ref[c, a, d] for c in range(COLS)], axis=0)

            @pl.when(a < BAND_ROWS)
            def _():
                band[a, :, (RADIUS + d) * block : (RADIUS + d + 1) * block] = whole

            if d > 0:

                @pl.when(a + d < BAND_ROWS)
                def _():
                    band[a + d, :, (RADIUS - d) * block : (RADIUS - d + 1) * block] = whole.T

        return carry

    lax.fori_loop(1, HELD, unfold, 0)

    def squares(k, carry):
        p = k + BEFORE - RADIUS
        for e in range(-SQUARE_REACH, SQUARE_REACH + 1):

            @pl.when(need[k, e + SQUARE_REACH] == 1)
            def _():
                width = (BAND - abs(e)) * block
                a, b = max(e, 0) * block, max(-e, 0) * block
                value = lax.dot_general(
                    band[p, :, a : a + width],
                    band[p + e, :, b : b + width],
                    (((1,), (1,)), ((), ())),
                    preferred_element_type=jnp.float32,
                )
                square[
                    p + e - 1, pl.ds(pl.multiple_of(k * block, block), block), :
                ] = value.astype(square.dtype)

        return carry

    lax.fori_loop(0, SQUARE_ROWS, squares, 0)

    def cubes(i, carry):
        left = band[i + BEFORE]
        rows = pl.ds(pl.multiple_of(i * block, block), BAND * block)
        mine = pl.ds(pl.multiple_of((i + RADIUS) * block, block), block)
        for t in range(0, targets.shape[1], 2):
            places = [place_of(i, t), place_of(i, t + 1)]
            right = jnp.concatenate([square[c, rows, :] for c in places], axis=1)
            cube = jnp.dot(left, right, preferred_element_type=jnp.float32)
            for n in range(2):
                own = square[places[n], mine, :].astype(jnp.float32)
                out_ref[i, t + n] = 3.0 * own - 2.0 * cube[:, n * block : (n + 1) * block]
        return carry

    lax.fori_loop(0, ROWS, cubes, 0)


def per_device(density, pattern, square_filter, cube_filter):
    n_layer = lax.axis_size("layer")
    total_rows = pattern.shape[0]
    rows, slots, part, block = density.shape
    first = (lax.axis_index("row") * n_layer + lax.axis_index("layer")) * ROWS
    first_row = first.astype(jnp.int32)[None]
    smem = pl.BlockSpec(memory_space=pltpu.SMEM)
    vmem = pl.BlockSpec(memory_space=pltpu.VMEM)
    anywhere = pl.BlockSpec(memory_space=pl.ANY)

    own_pattern = lax.dynamic_slice_in_dim(pattern, first, ROWS, 0)
    upper = pl.pallas_call(
        functools.partial(band_kernel, total_rows),
        out_shape=jax.ShapeDtypeStruct((ROWS, HALF, part, block), density.dtype),
        in_specs=[smem, smem, vmem],
        out_specs=vmem,
        name="band",
    )(first_row, own_pattern, density)

    held = pl.pallas_call(
        gather_kernel,
        out_shape=jax.ShapeDtypeStruct((COLS, HELD, HALF, part, block), density.dtype),
        in_specs=[anywhere],
        out_specs=anywhere,
        scratch_shapes=[
            pltpu.SemaphoreType.DMA((N_COPIES,)),
            pltpu.SemaphoreType.DMA((N_COPIES,)),
            pltpu.SemaphoreType.DMA,
        ],
        compiler_params=pltpu.CompilerParams(collective_id=0, has_side_effects=True),
        name="gather",
    )(upper)

    around = lax.rem(first - RADIUS + total_rows + jnp.arange(SQUARE_ROWS), total_rows)
    square_lists = jnp.take(square_filter, around, axis=0)
    share = cube_filter.shape[1] // COLS
    targets = lax.dynamic_slice(
        cube_filter, (first, lax.axis_index("col") * share), (ROWS, share)
    )
    return pl.pallas_call(
        functools.partial(product_kernel, total_rows, block),
        out_shape=jax.ShapeDtypeStruct((ROWS, share, block, block), jnp.float32),
        in_specs=[smem, smem, smem, vmem],
        out_specs=vmem,
        scratch_shapes=[
            pltpu.VMEM((BAND_ROWS, block, BAND * block), density.dtype),
            pltpu.VMEM((SQUARE_COLUMNS, SQUARE_ROWS * block, block), density.dtype),
            pltpu.SMEM((SQUARE_ROWS, 2 * SQUARE_REACH + 1), jnp.int32),
            pltpu.SMEM((SQUARE_ROWS, 2 * SQUARE_REACH + 1), jnp.int32),
        ],
        compiler_params=pltpu.CompilerParams(vmem_limit_bytes=60 << 20),
        name="product",
    )(first_row, square_lists, targets, held)


def solution(mesh):
    in_specs = (P(("row", "layer"), None, "col", None), P(), P(), P())
    out_specs = P(("row", "layer"), "col", None, None)
    return jax.shard_map(
        per_device, mesh=mesh, in_specs=in_specs, out_specs=out_specs, check_vma=False
    )
```

```python
import jax
import jax.numpy as jnp
from jax import lax
from jax.experimental import pallas as pl
from jax.experimental.pallas import tpu as pltpu
from jax.sharding import PartitionSpec as P

MESH = pl.DeviceIdType.MESH
RADIUS = 5
HALF = RADIUS + 1
BAND = 2 * RADIUS + 1
SQUARE_REACH = 2 * RADIUS
ROWS = 8
COLS = 4
BEFORE = 16


def block_list():
    within = [(i, d) for d in range(HALF) for i in range(ROWS - d)]
    near = [(i, d) for i, d in within if i < 2]
    tail = [(i, d) for i, d in within if i + d >= ROWS - 2]
    lower = [(i, -d) for i in range(RADIUS) for d in range(i + 1, HALF)]
    early = [b for b in within if b not in near and b not in tail]
    upper = [(i, d) for d in range(1, HALF) for i in range(ROWS - d, ROWS)]
    both = [b for b in tail if b in near]
    near = [b for b in near if b not in both]
    tail = [b for b in tail if b not in both]
    return lower + early + near + both + tail + upper


OWN = block_list()
LOWER = slice(0, 15)
WITHIN = slice(15, 48)
EDGE = slice(25, 37)
FAR = slice(36, 63)
N_OWN = len(OWN)
AT_ACROSS = N_OWN
AT_RELAY = AT_ACROSS + 33
AT_FAR = AT_RELAY + 33
AT_LOWER = AT_FAR + 27
AT_EDGE = AT_LOWER + 15
HELD = AT_EDGE + 12


def gather_kernel(pattern, density_ref, band_ref, upper, held, send, recv):
    row, col, layer = (lax.axis_index(a) for a in ("row", "col", "layer"))
    n_row, n_layer = lax.axis_size("row"), lax.axis_size("layer")
    side = lax.rem(layer, 2)
    up = lax.div(layer + 2, n_layer)
    down = 1 - lax.div(layer + n_layer - 2, n_layer)
    partner = {"layer": layer + 1 - 2 * side}
    after = {"row": lax.rem(row + up, n_row), "layer": lax.rem(layer + 2, n_layer)}
    before = {
        "row": lax.rem(row + n_row - down, n_row),
        "layer": lax.rem(layer + n_layer - 2, n_layer),
    }
    relay = {k: after[k] * (1 - side) + before[k] * side for k in after}
    right, left = lax.rem(col + 1, COLS), lax.rem(col + COLS - 1, COLS)
    block = density_ref.shape[-1]

    barrier = pltpu.get_barrier_semaphore()
    for peer in (partner, after, before, {"col": left}, {"col": right}):
        pl.semaphore_signal(barrier, inc=1, device_id=peer, device_id_type=MESH)

    slots, total_rows = pattern.shape
    first = (row * n_layer + layer) * ROWS
    columns = [[pattern[s, first + i] for s in range(slots)] for i in range(ROWS)]
    for n, (i, d) in enumerate(OWN):
        target = lax.rem(first + i + d + total_rows, total_rows)
        slot = jnp.int32(-1)
        for s in range(slots):
            slot = jnp.where(columns[i][s] == target, s, slot)
        found = density_ref[i, jnp.maximum(slot, 0)]
        upper[n] = jnp.where(slot >= 0, found, jnp.zeros_like(found))

    pl.semaphore_wait(barrier, 5)

    started, waited = [], set()

    def copy(src, dst, device):
        n = len(started)
        c = pltpu.make_async_remote_copy(
            src_ref=src,
            dst_ref=dst,
            send_sem=send.at[n],
            recv_sem=recv.at[n],
            device_id=device,
            device_id_type=MESH,
        )
        c.start()
        started.append(c)
        return c

    def arrived(c):
        if id(c) not in waited:
            c.wait_recv()
            waited.add(id(c))

    def spread(src, at, n):
        rows = pl.ds(at, n)
        return (
            copy(src, held.at[col, rows], {"col": right}),
            copy(src, held.at[col, rows], {"col": left}),
        )

    def forward(pair, at, n):
        half = n // 2
        arrived(pair[0])
        a = held.at[left, pl.ds(at, half)]
        first = copy(a, a, {"col": right})
        arrived(pair[1])
        b = held.at[right, pl.ds(at + half, n - half)]
        return first, copy(b, b, {"col": left})

    def sideways(at, n, from_y):
        rows = pl.ds(at, n)
        arrived(from_y[0])
        a = held.at[col, rows]
        first = copy(a, a, {"col": left})
        arrived(from_y[1])
        b = held.at[left, rows]
        return first, copy(b, b, {"col": right})

    def place(whole, p, d):
        at = RADIUS + d
        band_ref[p, :, at * block : (at + 1) * block] = whole
        if d:
            at = RADIUS - d
            band_ref[p + d, :, at * block : (at + 1) * block] = whole.T

    def unfold(at, blocks, base, own=None):
        for n, (i, d) in enumerate(blocks):
            parts = [held[c, at + n] for c in range(COLS)]
            place(jnp.concatenate(parts, axis=0), base + i, d)

    pieces = 3
    size = 33 // pieces
    seen = 24 - 16 * side
    seen_as = 8 + 16 * side
    own_parts = ((36, 27), (0, 36))
    across = [
        copy(
            upper.at[pl.ds(WITHIN.start + k * size, size)],
            held.at[col, pl.ds(AT_ACROSS + k * size, size)],
            partner,
        )
        for k in range(pieces)
    ]
    own_pairs = [spread(upper.at[pl.ds(at, n)], at, n) for at, n in own_parts]
    groups = (
        (FAR, AT_FAR, after),
        (LOWER, AT_LOWER, before),
        (EDGE, AT_EDGE, before),
    )
    first_slices = [
        copy(upper.at[g], held.at[col, pl.ds(at, g.stop - g.start)], device)
        for g, at, device in groups
    ]
    held[col, 0:N_OWN] = upper[...]
    arrived(own_pairs[0][0])
    arrived(own_pairs[1][0])
    second_slices = [
        copy(held.at[left, g], held.at[left, pl.ds(at, g.stop - g.start)], device)
        for g, at, device in groups
    ]
    own_last = [forward(p, at, n) for p, (at, n) in zip(own_pairs, own_parts)]
    side_last = [
        sideways(at, g.stop - g.start, (a, b))
        for (g, at, _), a, b in zip(groups, first_slices, second_slices)
    ]

    across_pairs, relay_first, relay_second, across_last, relay_last = [], [], [], [], []

    def take_across(k):
        arrived(across[k])
        at, put = AT_ACROSS + k * size, AT_RELAY + k * size
        src = held.at[col, pl.ds(at, size)]
        relay_first.append(copy(src, held.at[col, pl.ds(put, size)], relay))
        across_pairs.append(spread(src, at, size))

    def pass_on(k):
        at, put = AT_ACROSS + k * size, AT_RELAY + k * size
        arrived(across_pairs[k][0])
        src = held.at[left, pl.ds(at, size)]
        relay_second.append(copy(src, held.at[left, pl.ds(put, size)], relay))
        across_last.append(forward(across_pairs[k], at, size))

    for k in range(pieces):
        take_across(k)
        if k:
            pass_on(k - 1)
    for c in own_last[0]:
        arrived(c)
    pass_on(pieces - 1)
    for c in own_last[1]:
        arrived(c)
    unfold(0, OWN, BEFORE)
    for k in range(pieces):
        relay_last.append(
            sideways(AT_RELAY + k * size, size, (relay_first[k], relay_second[k]))
        )
    bases = (0, BEFORE + 2 * ROWS, BEFORE + 2 * ROWS)
    for (g, at, _), last, base in zip(groups, side_last, bases):
        for c in last:
            arrived(c)
        unfold(at, OWN[g], base)
    for group, at0, base in ((across_last, AT_ACROSS, seen), (relay_last, AT_RELAY, seen_as)):
        for k, last in enumerate(group):
            for c in last:
                arrived(c)
            at = WITHIN.start + k * size
            unfold(at0 + k * size, OWN[at : at + size], base)
    for c in started:
        arrived(c)
        c.wait_send()


N_COPIES = 47
BAND_ROWS = 39
SQUARE_ROWS = ROWS + 2 * RADIUS
SQUARE_COLUMNS = BAND_ROWS - 1


def product_kernel(
    square_lists, cube_lists, band, out_ref, square, member, need
):
    n_layer = lax.axis_size("layer")
    first = (lax.axis_index("row") * n_layer + lax.axis_index("layer")) * ROWS
    share, block = out_ref.shape[1:3]
    first_target = lax.axis_index("col") * share
    total_rows = square_lists.shape[1]
    offsets = 2 * SQUARE_REACH + 1

    def clear(k, carry):
        for e in range(offsets):
            member[k, e] = 0
            need[k, e] = 0
        return carry

    lax.fori_loop(0, SQUARE_ROWS, clear, 0)

    def listed(k, carry):
        row = lax.rem(first + k - RADIUS + total_rows, total_rows)
        for s in range(square_lists.shape[0]):
            e = square_lists[s, row] - row + SQUARE_REACH + total_rows
            member[k, lax.rem(e, total_rows)] = 1
        return carry

    lax.fori_loop(0, SQUARE_ROWS, listed, 0)

    def place_of(i, t):
        return lax.rem(
            cube_lists[first_target + t, first + i] - first + 3 * RADIUS + total_rows, total_rows
        )

    def wanted(i, carry):
        for t in range(share):
            place = place_of(i, t)
            for q in range(BAND):
                k = i + q
                e = place - 3 * RADIUS - (k - RADIUS) + SQUARE_REACH
                inside = (e >= 0) & (e < offsets)
                hit = inside & (member[k, jnp.clip(e, 0, offsets - 1)] == 1)

                @pl.when(hit)
                def _():
                    need[k, e] = 1

                @pl.when(jnp.logical_not(hit))
                def _():
                    square[place, pl.ds(pl.multiple_of(k * block, block), block), :] = (
                        jnp.zeros((block, block), square.dtype)
                    )

        return carry

    lax.fori_loop(0, ROWS, wanted, 0)

    def squares(k, carry):
        p = k + BEFORE - RADIUS
        for e in range(-SQUARE_REACH, SQUARE_REACH + 1):

            @pl.when(need[k, e + SQUARE_REACH] == 1)
            def _():
                width = (BAND - abs(e)) * block
                a, b = max(e, 0) * block, max(-e, 0) * block
                value = lax.dot_general(
                    band[p, :, a : a + width],
                    band[p + e, :, b : b + width],
                    (((1,), (1,)), ((), ())),
                    preferred_element_type=jnp.float32,
                )
                square[
                    p + e - 1, pl.ds(pl.multiple_of(k * block, block), block), :
                ] = value.astype(square.dtype)

        return carry

    lax.fori_loop(0, SQUARE_ROWS, squares, 0)

    def cubes(i, carry):
        left = band[i + BEFORE]
        rows = pl.ds(pl.multiple_of(i * block, block), BAND * block)
        mine = pl.ds(pl.multiple_of((i + RADIUS) * block, block), block)
        for t in range(0, share, 2):
            places = [place_of(i, t), place_of(i, t + 1)]
            right = jnp.concatenate([square[c, rows, :] for c in places], axis=1)
            cube = jnp.dot(left, right, preferred_element_type=jnp.float32)
            for n in range(2):
                own = square[places[n], mine, :].astype(jnp.float32)
                out_ref[i, t + n] = 3.0 * own - 2.0 * cube[:, n * block : (n + 1) * block]
        return carry

    lax.fori_loop(0, ROWS, cubes, 0)


def per_device(density, pattern, square_filter, cube_filter):
    part, block = density.shape[2:]
    share = cube_filter.shape[1] // COLS
    smem = pl.BlockSpec(memory_space=pltpu.SMEM)
    vmem = pl.BlockSpec(memory_space=pltpu.VMEM)

    band = pl.pallas_call(
        gather_kernel,
        out_shape=jax.ShapeDtypeStruct((BAND_ROWS, block, BAND * block), density.dtype),
        in_specs=[smem, vmem],
        out_specs=vmem,
        scratch_shapes=[
            pltpu.VMEM((N_OWN, part, block), density.dtype),
            pltpu.VMEM((COLS, HELD, part, block), density.dtype),
            pltpu.SemaphoreType.DMA((N_COPIES,)),
            pltpu.SemaphoreType.DMA((N_COPIES,)),
        ],
        compiler_params=pltpu.CompilerParams(
            collective_id=0, has_side_effects=True, vmem_limit_bytes=24 << 20
        ),
        name="gather",
    )(pattern.T, density)

    return pl.pallas_call(
        product_kernel,
        out_shape=jax.ShapeDtypeStruct((ROWS, share, block, block), jnp.float32),
        in_specs=[smem, smem, vmem],
        out_specs=vmem,
        scratch_shapes=[
            pltpu.VMEM((SQUARE_COLUMNS, SQUARE_ROWS * block, block), density.dtype),
            pltpu.SMEM((SQUARE_ROWS, 2 * SQUARE_REACH + 1), jnp.int32),
            pltpu.SMEM((SQUARE_ROWS, 2 * SQUARE_REACH + 1), jnp.int32),
        ],
        compiler_params=pltpu.CompilerParams(vmem_limit_bytes=28 << 20),
        name="product",
    )(square_filter.T, cube_filter.T, band)


def solution(mesh):
    in_specs = (P(("row", "layer"), None, "col", None), P(), P(), P())
    out_specs = P(("row", "layer"), "col", None, None)
    return jax.shard_map(
        per_device, mesh=mesh, in_specs=in_specs, out_specs=out_specs, check_vma=False
    )
```

```python
import jax
import jax.numpy as jnp
from jax import lax
from jax.experimental import pallas as pl
from jax.experimental.pallas import tpu as pltpu
from jax.sharding import PartitionSpec as P

MESH = pl.DeviceIdType.MESH
RADIUS = 5
HALF = RADIUS + 1
BAND = 2 * RADIUS + 1
SQUARE_REACH = 2 * RADIUS
ROWS = 8
COLS = 4
BEFORE = 16


def block_list():
    within = [(i, d) for d in range(HALF) for i in range(ROWS - d)]
    near = [(i, d) for i, d in within if i < 2]
    tail = [(i, d) for i, d in within if i + d >= ROWS - 2]
    lower = [(i, -d) for i in range(RADIUS) for d in range(i + 1, HALF)]
    early = [b for b in within if b not in near and b not in tail]
    upper = [(i, d) for d in range(1, HALF) for i in range(ROWS - d, ROWS)]
    both = [b for b in tail if b in near]
    near = [b for b in near if b not in both]
    tail = [b for b in tail if b not in both]
    return lower + early + near + both + tail + upper


OWN = block_list()
LOWER = slice(0, 15)
WITHIN = slice(15, 48)
EDGE = slice(25, 37)
FAR = slice(36, 63)
N_OWN = len(OWN)
AT_ACROSS = N_OWN
AT_RELAY = AT_ACROSS + 33
AT_FAR = AT_RELAY + 33
AT_LOWER = AT_FAR + 27
AT_EDGE = AT_LOWER + 15
HELD = AT_EDGE + 12


def gather_kernel(pattern, density_ref, band_ref, upper, held, send, recv):
    row, col, layer = (lax.axis_index(a) for a in ("row", "col", "layer"))
    n_row, n_layer = lax.axis_size("row"), lax.axis_size("layer")
    side = lax.rem(layer, 2)
    up = lax.div(layer + 2, n_layer)
    down = 1 - lax.div(layer + n_layer - 2, n_layer)
    partner = {"layer": layer + 1 - 2 * side}
    after = {"row": lax.rem(row + up, n_row), "layer": lax.rem(layer + 2, n_layer)}
    before = {
        "row": lax.rem(row + n_row - down, n_row),
        "layer": lax.rem(layer + n_layer - 2, n_layer),
    }
    relay = {k: after[k] * (1 - side) + before[k] * side for k in after}
    right, left = lax.rem(col + 1, COLS), lax.rem(col + COLS - 1, COLS)
    block = density_ref.shape[-1]

    barrier = pltpu.get_barrier_semaphore()
    for peer in (partner, after, before, {"col": left}, {"col": right}):
        pl.semaphore_signal(barrier, inc=1, device_id=peer, device_id_type=MESH)

    slots, total_rows = pattern.shape
    first = (row * n_layer + layer) * ROWS
    columns = [[pattern[s, first + i] for s in range(slots)] for i in range(ROWS)]
    for n, (i, d) in enumerate(OWN):
        target = lax.rem(first + i + d + total_rows, total_rows)
        slot = jnp.int32(-1)
        for s in range(slots):
            slot = jnp.where(columns[i][s] == target, s, slot)
        found = density_ref[i, jnp.maximum(slot, 0)]
        upper[n] = jnp.where(slot >= 0, found, jnp.zeros_like(found))

    pl.semaphore_wait(barrier, 5)

    started, waited = [], set()

    def copy(src, dst, device):
        n = len(started)
        c = pltpu.make_async_remote_copy(
            src_ref=src,
            dst_ref=dst,
            send_sem=send.at[n],
            recv_sem=recv.at[n],
            device_id=device,
            device_id_type=MESH,
        )
        c.start()
        started.append(c)
        return c

    def arrived(c):
        if id(c) not in waited:
            c.wait_recv()
            waited.add(id(c))

    def spread(src, at, n):
        rows = pl.ds(at, n)
        return (
            copy(src, held.at[col, rows], {"col": right}),
            copy(src, held.at[col, rows], {"col": left}),
        )

    def forward(pair, at, n):
        half = n // 2
        arrived(pair[0])
        a = held.at[left, pl.ds(at, half)]
        first = copy(a, a, {"col": right})
        arrived(pair[1])
        b = held.at[right, pl.ds(at + half, n - half)]
        return first, copy(b, b, {"col": left})

    def sideways(at, n, from_y):
        rows = pl.ds(at, n)
        arrived(from_y[0])
        a = held.at[col, rows]
        first = copy(a, a, {"col": left})
        arrived(from_y[1])
        b = held.at[left, rows]
        return first, copy(b, b, {"col": right})

    def place(whole, base, p, d):
        lane = (p % 2 + RADIUS + d) * block
        row = p % 2 * block
        band_ref[base + p // 2, row : row + block, lane : lane + block] = whole

    def unfold(at, blocks, base):
        for n, (i, d) in enumerate(blocks):
            parts = [held[c, at + n] for c in range(COLS)]
            whole = jnp.concatenate(parts, axis=0)
            place(whole, base, i, d)
            if d:
                place(whole.T, base, i + d, -d)

    pieces = 3
    size = 33 // pieces
    seen = 12 - 8 * side
    seen_as = 4 + 8 * side
    own_parts = ((36, 27), (0, 36))
    across = [
        copy(
            upper.at[pl.ds(WITHIN.start + k * size, size)],
            held.at[col, pl.ds(AT_ACROSS + k * size, size)],
            partner,
        )
        for k in range(pieces)
    ]
    own_pairs = [spread(upper.at[pl.ds(at, n)], at, n) for at, n in own_parts]
    groups = (
        (FAR, AT_FAR, after),
        (LOWER, AT_LOWER, before),
        (EDGE, AT_EDGE, before),
    )
    first_slices = [
        copy(upper.at[g], held.at[col, pl.ds(at, g.stop - g.start)], device)
        for g, at, device in groups
    ]
    held[col, 0:N_OWN] = upper[...]
    for n in range(BAND_PAIRS):
        if 5 <= n < 15:
            corner = jnp.zeros((block, block), band_ref.dtype)
            band_ref[n, 0:block, BAND * block :] = corner
            band_ref[n, block:, 0:block] = corner
        else:
            band_ref[n] = jnp.zeros_like(band_ref[n])
    arrived(own_pairs[0][0])
    arrived(own_pairs[1][0])
    second_slices = [
        copy(held.at[left, g], held.at[left, pl.ds(at, g.stop - g.start)], device)
        for g, at, device in groups
    ]
    own_last = [forward(p, at, n) for p, (at, n) in zip(own_pairs, own_parts)]
    side_last = [
        sideways(at, g.stop - g.start, (a, b))
        for (g, at, _), a, b in zip(groups, first_slices, second_slices)
    ]

    across_pairs, relay_first, relay_second, across_last, relay_last = [], [], [], [], []

    def take_across(k):
        arrived(across[k])
        at, put = AT_ACROSS + k * size, AT_RELAY + k * size
        src = held.at[col, pl.ds(at, size)]
        relay_first.append(copy(src, held.at[col, pl.ds(put, size)], relay))
        across_pairs.append(spread(src, at, size))

    def pass_on(k):
        at, put = AT_ACROSS + k * size, AT_RELAY + k * size
        arrived(across_pairs[k][0])
        src = held.at[left, pl.ds(at, size)]
        relay_second.append(copy(src, held.at[left, pl.ds(put, size)], relay))
        across_last.append(forward(across_pairs[k], at, size))

    for k in range(pieces):
        take_across(k)
        if k:
            pass_on(k - 1)
    for c in own_last[0]:
        arrived(c)
    pass_on(pieces - 1)
    for c in own_last[1]:
        arrived(c)
    unfold(0, OWN, BEFORE // 2)
    for k in range(pieces):
        relay_last.append(
            sideways(AT_RELAY + k * size, size, (relay_first[k], relay_second[k]))
        )
    bases = (0, BEFORE // 2 + ROWS, BEFORE // 2 + ROWS)
    for (g, at, _), last, base in zip(groups, side_last, bases):
        for c in last:
            arrived(c)
        unfold(at, OWN[g], base)
    for group, at0, base in ((across_last, AT_ACROSS, seen), (relay_last, AT_RELAY, seen_as)):
        for k, last in enumerate(group):
            for c in last:
                arrived(c)
            at = WITHIN.start + k * size
            unfold(at0 + k * size, OWN[at : at + size], base)
    for c in started:
        arrived(c)
        c.wait_send()


N_COPIES = 47
BAND_PAIRS = 20
SQUARE_PAIRS = 10
WIDTH = BAND + 1


def product_kernel(square_lists, cube_lists, band, out_ref, square, member):
    n_layer = lax.axis_size("layer")
    first = (lax.axis_index("row") * n_layer + lax.axis_index("layer")) * ROWS
    share, block = out_ref.shape[1:3]
    first_target = lax.axis_index("col") * share
    total_rows = square_lists.shape[1]
    reach = SQUARE_REACH + 1

    def listed(k, carry):
        for e in range(2 * reach + 1):
            member[k, e] = 0
        row = lax.rem(first + k - RADIUS - 1 + total_rows, total_rows)
        for s in range(square_lists.shape[0]):
            e = square_lists[s, row] - row + reach + total_rows
            member[k, lax.rem(e, total_rows)] = 1
        return carry

    lax.fori_loop(0, 2 * SQUARE_PAIRS, listed, 0)

    for j in range(BAND_PAIRS):
        for k in range(SQUARE_PAIRS):
            if abs(j - k - 5) > RADIUS:
                for h in range(2):
                    square[2 * j + h, 2 * k * block : 2 * (k + 1) * block, :] = jnp.zeros(
                        (2 * block, block), square.dtype
                    )

    def squares(k, carry):
        for e in range(-RADIUS, RADIUS + 1):
            width = (WIDTH - 2 * abs(e)) * block
            a, b = max(2 * e, 0) * block, max(-2 * e, 0) * block
            value = lax.dot_general(
                band[k + 5, :, a : a + width],
                band[k + 5 + e, :, b : b + width],
                (((1,), (1,)), ((), ())),
                preferred_element_type=jnp.float32,
            )
            for hj in range(2):
                for hk in range(2):
                    kept = member[2 * k + hk, 2 * e + hj - hk + reach] == 1
                    part = value[hk * block : (hk + 1) * block, hj * block : (hj + 1) * block]
                    row = pl.multiple_of((2 * k + hk) * block, block)
                    square[2 * (k + 5 + e) + hj, pl.ds(row, block), :] = jnp.where(
                        kept, part, 0.0
                    ).astype(square.dtype)
        return carry

    lax.fori_loop(0, SQUARE_PAIRS, squares, 0)

    def cubes(n, carry):
        for h in range(2):
            i = 2 * n + h
            left = band[n + BEFORE // 2, h * block : (h + 1) * block, h * block : (h + BAND) * block]
            rows = pl.ds(pl.multiple_of((i + 1) * block, block), BAND * block)
            mine = pl.ds(pl.multiple_of((i + 1 + RADIUS) * block, block), block)
            places = [
                lax.rem(
                    cube_lists[first_target + t, first + i] - first + BEFORE + total_rows,
                    total_rows,
                )
                for t in range(share)
            ]
            right = jnp.concatenate([square[c, rows, :] for c in places], axis=1)
            cube = jnp.dot(left, right, preferred_element_type=jnp.float32)
            for t, c in enumerate(places):
                own = square[c, mine, :].astype(jnp.float32)
                out_ref[i, t] = 3.0 * own - 2.0 * cube[:, t * block : (t + 1) * block]
        return carry

    lax.fori_loop(0, ROWS // 2, cubes, 0)


def per_device(density, pattern, square_filter, cube_filter):
    part, block = density.shape[2:]
    share = cube_filter.shape[1] // COLS
    smem = pl.BlockSpec(memory_space=pltpu.SMEM)
    vmem = pl.BlockSpec(memory_space=pltpu.VMEM)

    band = pl.pallas_call(
        gather_kernel,
        out_shape=jax.ShapeDtypeStruct((BAND_PAIRS, 2 * block, WIDTH * block), density.dtype),
        in_specs=[smem, vmem],
        out_specs=vmem,
        scratch_shapes=[
            pltpu.VMEM((N_OWN, part, block), density.dtype),
            pltpu.VMEM((COLS, HELD, part, block), density.dtype),
            pltpu.SemaphoreType.DMA((N_COPIES,)),
            pltpu.SemaphoreType.DMA((N_COPIES,)),
        ],
        compiler_params=pltpu.CompilerParams(
            collective_id=0, has_side_effects=True, vmem_limit_bytes=24 << 20
        ),
        name="gather",
    )(pattern.T, density)

    return pl.pallas_call(
        product_kernel,
        out_shape=jax.ShapeDtypeStruct((ROWS, share, block, block), jnp.float32),
        in_specs=[smem, smem, vmem],
        out_specs=vmem,
        scratch_shapes=[
            pltpu.VMEM((2 * BAND_PAIRS, 2 * SQUARE_PAIRS * block, block), density.dtype),
            pltpu.SMEM((2 * SQUARE_PAIRS, 2 * SQUARE_REACH + 3), jnp.int32),
        ],
        compiler_params=pltpu.CompilerParams(vmem_limit_bytes=31 << 20),
        name="product",
    )(square_filter.T, cube_filter.T, band)


def solution(mesh):
    in_specs = (P(("row", "layer"), None, "col", None), P(), P(), P())
    out_specs = P(("row", "layer"), "col", None, None)
    return jax.shard_map(
        per_device, mesh=mesh, in_specs=in_specs, out_specs=out_specs, check_vma=False
    )
```

```python
import jax
import jax.numpy as jnp
from jax import lax
from jax.experimental import pallas as pl
from jax.experimental.pallas import tpu as pltpu
from jax.sharding import PartitionSpec as P

MESH = pl.DeviceIdType.MESH
RADIUS = 5
HALF = RADIUS + 1
BAND = 2 * RADIUS + 1
SQUARE_REACH = 2 * RADIUS
ROWS = 8
COLS = 4
BEFORE = 16


BAND_PAIRS = 20
SQUARE_PAIRS = 10
WIDTH = BAND + 1


def block_list():
    within = [(i, d) for d in range(HALF) for i in range(ROWS - d)]
    near = [(i, d) for i, d in within if i < 2]
    tail = [(i, d) for i, d in within if i + d >= ROWS - 2]
    lower = [(i, -d) for i in range(RADIUS) for d in range(i + 1, HALF)]
    early = [b for b in within if b not in near and b not in tail]
    upper = [(i, d) for d in range(1, HALF) for i in range(ROWS - d, ROWS)]
    both = [b for b in tail if b in near]
    near = [b for b in near if b not in both]
    tail = [b for b in tail if b not in both]
    return lower + early + near + both + tail + upper


OWN = block_list()
LOWER = slice(0, 15)
WITHIN = slice(15, 48)
EDGE = slice(25, 37)
FAR = slice(36, 63)
N_OWN = len(OWN)
AT_ACROSS = N_OWN
AT_RELAY = AT_ACROSS + 33
AT_FAR = AT_RELAY + 33
AT_LOWER = AT_FAR + 27
AT_EDGE = AT_LOWER + 15
HELD = AT_EDGE + 12


def purify_kernel(
    pattern,
    square_lists,
    cube_lists,
    density_ref,
    out_ref,
    band_ref,
    square,
    upper,
    held,
    member,
    send,
    recv,
):
    row, col, layer = (lax.axis_index(a) for a in ("row", "col", "layer"))
    n_row, n_layer = lax.axis_size("row"), lax.axis_size("layer")
    side = lax.rem(layer, 2)
    up = lax.div(layer + 2, n_layer)
    down = 1 - lax.div(layer + n_layer - 2, n_layer)
    partner = {"layer": layer + 1 - 2 * side}
    after = {"row": lax.rem(row + up, n_row), "layer": lax.rem(layer + 2, n_layer)}
    before = {
        "row": lax.rem(row + n_row - down, n_row),
        "layer": lax.rem(layer + n_layer - 2, n_layer),
    }
    relay = {k: after[k] * (1 - side) + before[k] * side for k in after}
    right, left = lax.rem(col + 1, COLS), lax.rem(col + COLS - 1, COLS)
    block = density_ref.shape[-1]

    barrier = pltpu.get_barrier_semaphore()
    for peer in (partner, after, before, {"col": left}, {"col": right}):
        pl.semaphore_signal(barrier, inc=1, device_id=peer, device_id_type=MESH)

    slots, total_rows = pattern.shape
    first = (row * n_layer + layer) * ROWS

    def take_own(blocks):
        for n in range(blocks.start, blocks.stop):
            i, d = OWN[n]
            target = lax.rem(first + i + d + total_rows, total_rows)
            slot = jnp.int32(-1)
            for s in range(slots):
                slot = jnp.where(pattern[s, first + i] == target, s, slot)
            found = density_ref[i, jnp.maximum(slot, 0)]
            upper[n] = jnp.where(slot >= 0, found, jnp.zeros_like(found))

    take_own(WITHIN)
    pl.semaphore_wait(barrier, 5)

    started, waited = [], set()

    def copy(src, dst, device):
        n = len(started)
        c = pltpu.make_async_remote_copy(
            src_ref=src,
            dst_ref=dst,
            send_sem=send.at[n],
            recv_sem=recv.at[n],
            device_id=device,
            device_id_type=MESH,
        )
        c.start()
        started.append(c)
        return c

    def arrived(c):
        if id(c) not in waited:
            c.wait_recv()
            waited.add(id(c))

    def spread(src, at, n):
        rows = pl.ds(at, n)
        return (
            copy(src, held.at[col, rows], {"col": right}),
            copy(src, held.at[col, rows], {"col": left}),
        )

    def forward(pair, at, n):
        half = n // 2
        arrived(pair[0])
        a = held.at[left, pl.ds(at, half)]
        first = copy(a, a, {"col": right})
        arrived(pair[1])
        b = held.at[right, pl.ds(at + half, n - half)]
        return first, copy(b, b, {"col": left})

    def sideways(at, n, from_y):
        rows = pl.ds(at, n)
        arrived(from_y[0])
        a = held.at[col, rows]
        first = copy(a, a, {"col": left})
        arrived(from_y[1])
        b = held.at[left, rows]
        return first, copy(b, b, {"col": right})

    def place(whole, base, p, d):
        lane = (p % 2 + RADIUS + d) * block
        row = p % 2 * block
        band_ref[base + p // 2, row : row + block, lane : lane + block] = whole

    def unfold(at, blocks, base):
        for n, (i, d) in enumerate(blocks):
            parts = [held[c, at + n] for c in range(COLS)]
            whole = jnp.concatenate(parts, axis=0)
            place(whole, base, i, d)
            if d:
                place(whole.T, base, i + d, -d)

    pieces = 3
    size = 33 // pieces
    seen = 12 - 8 * side
    seen_as = 4 + 8 * side
    own_parts = ((36, 27), (0, 36))
    across = [
        copy(
            upper.at[pl.ds(WITHIN.start + k * size, size)],
            held.at[col, pl.ds(AT_ACROSS + k * size, size)],
            partner,
        )
        for k in range(pieces)
    ]
    take_own(slice(WITHIN.stop, N_OWN))
    take_own(LOWER)
    own_pairs = [spread(upper.at[pl.ds(at, n)], at, n) for at, n in own_parts]
    groups = (
        (FAR, AT_FAR, after),
        (LOWER, AT_LOWER, before),
        (EDGE, AT_EDGE, before),
    )
    first_slices = [
        copy(upper.at[g], held.at[col, pl.ds(at, g.stop - g.start)], device)
        for g, at, device in groups
    ]
    held[col, 0:N_OWN] = upper[...]
    for n in range(BAND_PAIRS):
        if 5 <= n < 15:
            corner = jnp.zeros((block, block), band_ref.dtype)
            band_ref[n, 0:block, BAND * block :] = corner
            band_ref[n, block:, 0:block] = corner
        else:
            band_ref[n] = jnp.zeros_like(band_ref[n])
    for j in range(BAND_PAIRS):
        for k in range(SQUARE_PAIRS):
            if abs(j - k - 5) > RADIUS:
                for h in range(2):
                    square[2 * j + h, 2 * k * block : 2 * (k + 1) * block, :] = jnp.zeros(
                        (2 * block, block), square.dtype
                    )
    reach = SQUARE_REACH + 1

    def table(k, carry):
        at = lax.rem(first + k - RADIUS - 1 + total_rows, total_rows)
        listed = [square_lists[s, at] for s in range(square_lists.shape[0])]
        for e in range(2 * reach + 1):
            target = lax.rem(at + e - reach + total_rows, total_rows)
            kept = jnp.int32(0)
            for one in listed:
                kept = jnp.where(one == target, 1, kept)
            member[k, e] = kept
        return carry

    lax.fori_loop(0, 2 * SQUARE_PAIRS, table, 0)

    def square_pair(k, e):
        width = (WIDTH - 2 * abs(e)) * block
        a, b = max(2 * e, 0) * block, max(-2 * e, 0) * block
        value = lax.dot_general(
            band_ref[k, :, a : a + width],
            band_ref[k + e, :, b : b + width],
            (((1,), (1,)), ((), ())),
            preferred_element_type=jnp.float32,
        )
        for hj in range(2):
            for hk in range(2):
                at = 2 * (k - 5) + hk
                kept = member[at, 2 * e + hj - hk + reach] == 1
                part = value[hk * block : (hk + 1) * block, hj * block : (hj + 1) * block]
                rows = pl.ds(pl.multiple_of(at * block, block), block)
                square[2 * (k + e) + hj, rows, :] = jnp.where(kept, part, 0.0).astype(
                    square.dtype
                )

    def square_rows(k, carry):
        for e in range(-RADIUS, RADIUS + 1):
            square_pair(k, e)
        return carry
    arrived(own_pairs[0][0])
    arrived(own_pairs[1][0])
    second_slices = [
        copy(held.at[left, g], held.at[left, pl.ds(at, g.stop - g.start)], device)
        for g, at, device in groups
    ]
    own_last = [forward(p, at, n) for p, (at, n) in zip(own_pairs, own_parts)]
    side_last = [
        sideways(at, g.stop - g.start, (a, b))
        for (g, at, _), a, b in zip(groups, first_slices, second_slices)
    ]

    across_pairs, relay_first, relay_second, across_last, relay_last = [], [], [], [], []

    def take_across(k):
        arrived(across[k])
        at, put = AT_ACROSS + k * size, AT_RELAY + k * size
        src = held.at[col, pl.ds(at, size)]
        relay_first.append(copy(src, held.at[col, pl.ds(put, size)], relay))
        across_pairs.append(spread(src, at, size))

    def pass_on(k):
        at, put = AT_ACROSS + k * size, AT_RELAY + k * size
        arrived(across_pairs[k][0])
        src = held.at[left, pl.ds(at, size)]
        relay_second.append(copy(src, held.at[left, pl.ds(put, size)], relay))
        across_last.append(forward(across_pairs[k], at, size))

    for k in range(pieces):
        take_across(k)
        if k:
            pass_on(k - 1)
    for c in own_last[0]:
        arrived(c)
    for c in own_last[1]:
        arrived(c)
    unfold(0, OWN[0:36], BEFORE // 2)
    pass_on(pieces - 1)
    unfold(36, OWN[36:], BEFORE // 2)

    def unfold_piece(at0, k, last, base):
        for c in last:
            arrived(c)
        at = WITHIN.start + k * size
        unfold(at0 + k * size, OWN[at : at + size], base)

    bases = (0, BEFORE // 2 + ROWS, BEFORE // 2 + ROWS)
    for k in range(pieces):
        at = AT_RELAY + k * size
        relay_last.append(sideways(at, size, (relay_first[k], relay_second[k])))
        g, at, _ = groups[k]
        for c in side_last[k]:
            arrived(c)
        unfold(at, OWN[g], bases[k])
    for k in range(pieces):
        unfold_piece(AT_ACROSS, k, across_last[k], seen)

    lax.fori_loop(8 - 3 * side, 15 - 3 * side, square_rows, 0)
    for k in range(pieces):
        unfold_piece(AT_RELAY, k, relay_last[k], seen_as)
    lax.fori_loop(5 + 7 * side, 8 + 7 * side, square_rows, 0)
    again = [(k, j) for k in range(8, 13) for j in range(max(4, k - RADIUS), 8)]
    for which in range(2):

        @pl.when(side == which)
        def _():
            for k, j in again:
                square_pair(19 - k if which else k, k - j if which else j - k)

    share = out_ref.shape[1]
    first_target = col * share

    def cubes(n, carry):
        for h in range(2):
            i = 2 * n + h
            left = band_ref[n + BEFORE // 2, h * block : (h + 1) * block, h * block : (h + BAND) * block]
            rows = pl.ds(pl.multiple_of((i + 1) * block, block), BAND * block)
            mine = pl.ds(pl.multiple_of((i + 1 + RADIUS) * block, block), block)
            places = [
                jnp.minimum(
                    lax.rem(
                        cube_lists[first_target + t, first + i] - first + BEFORE + total_rows,
                        total_rows,
                    ),
                    2 * BAND_PAIRS - 1,
                )
                for t in range(share)
            ]
            right = jnp.concatenate([square[c, rows, :] for c in places], axis=1)
            cube = jnp.dot(left, right, preferred_element_type=jnp.float32)
            for t, c in enumerate(places):
                own = square[c, mine, :].astype(jnp.float32)
                out_ref[i, t] = 3.0 * own - 2.0 * cube[:, t * block : (t + 1) * block]
        return carry

    lax.fori_loop(0, ROWS // 2, cubes, 0)

    for c in started:
        arrived(c)
        c.wait_send()


N_COPIES = 47
def per_device(density, pattern, square_filter, cube_filter):
    part, block = density.shape[2:]
    share = cube_filter.shape[1] // COLS
    smem = pl.BlockSpec(memory_space=pltpu.SMEM)
    vmem = pl.BlockSpec(memory_space=pltpu.VMEM)

    return pl.pallas_call(
        purify_kernel,
        out_shape=jax.ShapeDtypeStruct((ROWS, share, block, block), jnp.float32),
        in_specs=[smem, smem, smem, vmem],
        out_specs=vmem,
        scratch_shapes=[
            pltpu.VMEM((BAND_PAIRS, 2 * block, WIDTH * block), density.dtype),
            pltpu.VMEM((2 * BAND_PAIRS, 2 * SQUARE_PAIRS * block, block), density.dtype),
            pltpu.VMEM((N_OWN, part, block), density.dtype),
            pltpu.VMEM((COLS, HELD, part, block), density.dtype),
            pltpu.SMEM((2 * SQUARE_PAIRS, 2 * SQUARE_REACH + 3), jnp.int32),
            pltpu.SemaphoreType.DMA((N_COPIES,)),
            pltpu.SemaphoreType.DMA((N_COPIES,)),
        ],
        compiler_params=pltpu.CompilerParams(
            collective_id=0, has_side_effects=True, vmem_limit_bytes=54 << 20
        ),
        name="purify",
    )(pattern.T, square_filter.T, cube_filter.T, density)


def solution(mesh):
    in_specs = (P(("row", "layer"), None, "col", None), P(), P(), P())
    out_specs = P(("row", "layer"), "col", None, None)
    return jax.shard_map(
        per_device, mesh=mesh, in_specs=in_specs, out_specs=out_specs, check_vma=False
    )
```

```python
import jax
import jax.numpy as jnp
from jax import lax
from jax.experimental import pallas as pl
from jax.experimental.pallas import tpu as pltpu
from jax.sharding import PartitionSpec as P

MESH = pl.DeviceIdType.MESH
RADIUS = 5
HALF = RADIUS + 1
BAND = 2 * RADIUS + 1
SQUARE_REACH = 2 * RADIUS
ROWS = 8
COLS = 4
BEFORE = 16


BAND_PAIRS = 20
SQUARE_PAIRS = 10
WIDTH = BAND + 1


def block_list():
    within = [(i, d) for d in range(HALF) for i in range(ROWS - d)]
    near = [(i, d) for i, d in within if i < 2]
    tail = [(i, d) for i, d in within if i + d >= ROWS - 2]
    lower = [(i, -d) for i in range(RADIUS) for d in range(i + 1, HALF)]
    early = [b for b in within if b not in near and b not in tail]
    upper = [(i, d) for d in range(1, HALF) for i in range(ROWS - d, ROWS)]
    both = [b for b in tail if b in near]
    near = [b for b in near if b not in both]
    tail = [b for b in tail if b not in both]
    return lower + early + near + both + tail + upper


OWN = block_list()
LOWER = slice(0, 15)
WITHIN = slice(15, 48)
EDGE = slice(25, 37)
FAR = slice(36, 63)
N_OWN = len(OWN)
AT_ACROSS = N_OWN
AT_RELAY = AT_ACROSS + 33
AT_FAR = AT_RELAY + 33
AT_LOWER = AT_FAR + 27
AT_EDGE = AT_LOWER + 15
HELD = AT_EDGE + 12


def purify_kernel(
    pattern,
    square_lists,
    cube_lists,
    density_ref,
    out_ref,
    band_ref,
    square,
    upper,
    held,
    member,
    send,
    recv,
):
    row, col, layer = (lax.axis_index(a) for a in ("row", "col", "layer"))
    n_row, n_layer = lax.axis_size("row"), lax.axis_size("layer")
    side = lax.rem(layer, 2)
    up = lax.div(layer + 2, n_layer)
    down = 1 - lax.div(layer + n_layer - 2, n_layer)
    partner = {"layer": layer + 1 - 2 * side}
    after = {"row": lax.rem(row + up, n_row), "layer": lax.rem(layer + 2, n_layer)}
    before = {
        "row": lax.rem(row + n_row - down, n_row),
        "layer": lax.rem(layer + n_layer - 2, n_layer),
    }
    relay = {k: after[k] * (1 - side) + before[k] * side for k in after}
    right, left = lax.rem(col + 1, COLS), lax.rem(col + COLS - 1, COLS)
    block = density_ref.shape[-1]

    barrier = pltpu.get_barrier_semaphore()
    for peer in (partner, after, before, {"col": left}, {"col": right}):
        pl.semaphore_signal(barrier, inc=1, device_id=peer, device_id_type=MESH)

    slots, total_rows = pattern.shape
    first = (row * n_layer + layer) * ROWS

    def take_own(blocks):
        for n in range(blocks.start, blocks.stop):
            i, d = OWN[n]
            target = lax.rem(first + i + d + total_rows, total_rows)
            slot = jnp.int32(-1)
            for s in range(slots):
                slot = jnp.where(pattern[s, first + i] == target, s, slot)
            found = density_ref[i, jnp.maximum(slot, 0)]
            upper[n] = jnp.where(slot >= 0, found, jnp.zeros_like(found))

    take_own(WITHIN)
    pl.semaphore_wait(barrier, 5)

    started, waited = [], set()

    def copy(src, dst, device):
        n = len(started)
        c = pltpu.make_async_remote_copy(
            src_ref=src,
            dst_ref=dst,
            send_sem=send.at[n],
            recv_sem=recv.at[n],
            device_id=device,
            device_id_type=MESH,
        )
        c.start()
        started.append(c)
        return c

    def arrived(c):
        if id(c) not in waited:
            c.wait_recv()
            waited.add(id(c))

    def spread(src, at, n):
        rows = pl.ds(at, n)
        return (
            copy(src, held.at[col, rows], {"col": right}),
            copy(src, held.at[col, rows], {"col": left}),
        )

    def forward(pair, at, n):
        half = n // 2
        arrived(pair[0])
        a = held.at[left, pl.ds(at, half)]
        first = copy(a, a, {"col": right})
        arrived(pair[1])
        b = held.at[right, pl.ds(at + half, n - half)]
        return first, copy(b, b, {"col": left})

    def sideways(at, n, from_y):
        rows = pl.ds(at, n)
        arrived(from_y[0])
        a = held.at[col, rows]
        first = copy(a, a, {"col": left})
        arrived(from_y[1])
        b = held.at[left, rows]
        return first, copy(b, b, {"col": right})

    def place(whole, base, p, d):
        lane = (p % 2 + RADIUS + d) * block
        row = p % 2 * block
        band_ref[base + p // 2, row : row + block, lane : lane + block] = whole

    def unfold(at, blocks, base):
        for n, (i, d) in enumerate(blocks):
            parts = [held[c, at + n] for c in range(COLS)]
            whole = jnp.concatenate(parts, axis=0)
            place(whole, base, i, d)
            if d:
                place(whole.T, base, i + d, -d)

    pieces = 3
    size = 33 // pieces
    seen = 12 - 8 * side
    seen_as = 4 + 8 * side
    own_parts = ((36, 27), (0, 36))
    across = [
        copy(
            upper.at[pl.ds(WITHIN.start + k * size, size)],
            held.at[col, pl.ds(AT_ACROSS + k * size, size)],
            partner,
        )
        for k in range(pieces)
    ]
    take_own(slice(WITHIN.stop, N_OWN))
    take_own(LOWER)
    own_pairs = [spread(upper.at[pl.ds(at, n)], at, n) for at, n in own_parts]
    groups = (
        (FAR, AT_FAR, after),
        (LOWER, AT_LOWER, before),
        (EDGE, AT_EDGE, before),
    )
    first_slices = [
        copy(upper.at[g], held.at[col, pl.ds(at, g.stop - g.start)], device)
        for g, at, device in groups
    ]
    held[col, 0:N_OWN] = upper[...]

    def zero_band():
        for n in range(BAND_PAIRS):
            if 5 <= n < 15:
                corner = jnp.zeros((block, block), band_ref.dtype)
                band_ref[n, 0:block, BAND * block :] = corner
                band_ref[n, block:, 0:block] = corner
            else:
                band_ref[n] = jnp.zeros_like(band_ref[n])

    def zero_square():
        for j in range(BAND_PAIRS):
            for k in range(SQUARE_PAIRS):
                if abs(j - k - 5) > RADIUS:
                    for h in range(2):
                        square[2 * j + h, 2 * k * block : 2 * (k + 1) * block, :] = jnp.zeros(
                            (2 * block, block), square.dtype
                        )

    reach = SQUARE_REACH + 1

    def table(k, carry):
        at = lax.rem(first + k - RADIUS - 1 + total_rows, total_rows)
        listed = [square_lists[s, at] for s in range(square_lists.shape[0])]
        for e in range(2 * reach + 1):
            target = lax.rem(at + e - reach + total_rows, total_rows)
            kept = jnp.int32(0)
            for one in listed:
                kept = jnp.where(one == target, 1, kept)
            member[k, e] = kept
        return carry

    def square_pair(k, j, e, a, b):
        width = (WIDTH - 2 * abs(e)) * block
        turned = (j - k) * 2 + reach
        value = lax.dot_general(
            band_ref[k, :, pl.ds(pl.multiple_of(a, block), width)],
            band_ref[j, :, pl.ds(pl.multiple_of(b, block), width)],
            (((1,), (1,)), ((), ())),
            preferred_element_type=jnp.float32,
        )
        for hj in range(2):
            for hk in range(2):
                at = 2 * (k - 5) + hk
                kept = member[at, turned + hj - hk] == 1
                part = value[hk * block : (hk + 1) * block, hj * block : (hj + 1) * block]
                rows = pl.ds(pl.multiple_of(at * block, block), block)
                square[2 * j + hj, rows, :] = jnp.where(kept, part, 0.0).astype(square.dtype)

    def straight(k, e):
        square_pair(k, k + e, e, max(2 * e, 0) * block, max(-2 * e, 0) * block)

    def square_rows(k, carry):
        for e in range(-RADIUS, RADIUS + 1):
            straight(k, e)
        return carry

    def mirrored(k, j):
        e = j - k
        a, b = max(2 * e, 0) * block, max(-2 * e, 0) * block
        square_pair(
            k + side * (19 - 2 * k), j + side * (19 - 2 * j), e, a + side * (b - a), b + side * (a - b)
        )

    zero_band()
    arrived(own_pairs[0][0])

    def second(n):
        g, at, device = groups[n]
        return copy(held.at[left, g], held.at[left, pl.ds(at, g.stop - g.start)], device)

    second_slices = [second(0)]
    lax.fori_loop(0, 2 * SQUARE_PAIRS, table, 0)
    arrived(own_pairs[1][0])
    second_slices += [second(1), second(2)]
    own_last = [forward(p, at, n) for p, (at, n) in zip(own_pairs, own_parts)]
    zero_square()

    across_pairs, relay_first, relay_second, across_last, relay_last = [], [], [], [], []

    def take_across(k):
        arrived(across[k])
        at, put = AT_ACROSS + k * size, AT_RELAY + k * size
        src = held.at[col, pl.ds(at, size)]
        relay_first.append(copy(src, held.at[col, pl.ds(put, size)], relay))
        across_pairs.append(spread(src, at, size))

    def pass_on(k):
        at, put = AT_ACROSS + k * size, AT_RELAY + k * size
        arrived(across_pairs[k][0])
        src = held.at[left, pl.ds(at, size)]
        relay_second.append(copy(src, held.at[left, pl.ds(put, size)], relay))
        across_last.append(forward(across_pairs[k], at, size))

    def unfold_piece(at0, k, last, base):
        for c in last:
            arrived(c)
        at = WITHIN.start + k * size
        unfold(at0 + k * size, OWN[at : at + size], base)

    take_across(0)
    for n in range(2):
        at, count = own_parts[n]
        for c in own_last[n]:
            arrived(c)
        unfold(at, OWN[at : at + count], BEFORE // 2)
    take_across(1)
    pass_on(0)
    side_last = [
        sideways(at, g.stop - g.start, (a, b))
        for (g, at, _), a, b in zip(groups, first_slices, second_slices)
    ]

    for k in range(8, 12):
        for j in range(8, 12):
            straight(k, j - k)

    take_across(2)
    pass_on(1)
    pass_on(2)
    bases = (0, BEFORE // 2 + ROWS, BEFORE // 2 + ROWS)
    for k in range(pieces):
        g, at, _ = groups[k]
        for c in side_last[k]:
            arrived(c)
        unfold(at, OWN[g], bases[k])
        at = AT_RELAY + k * size
        relay_last.append(sideways(at, size, (relay_first[k], relay_second[k])))
    for k in range(pieces):
        unfold_piece(AT_ACROSS, k, across_last[k], seen)

    lax.fori_loop(12 - 7 * side, 15 - 7 * side, square_rows, 0)
    for k in range(8, 12):
        for j in range(k - RADIUS, k + RADIUS + 1):
            if not 4 <= j < 12:
                mirrored(k, j)
    for k in range(pieces):
        unfold_piece(AT_RELAY, k, relay_last[k], seen_as)
    lax.fori_loop(5 + 7 * side, 8 + 7 * side, square_rows, 0)
    for k in range(8, 13):
        for j in range(max(4, k - RADIUS), 8):
            mirrored(k, j)

    share = out_ref.shape[1]
    first_target = col * share

    def cubes(n, carry):
        for h in range(2):
            i = 2 * n + h
            left = band_ref[n + BEFORE // 2, h * block : (h + 1) * block, h * block : (h + BAND) * block]
            rows = pl.ds(pl.multiple_of((i + 1) * block, block), BAND * block)
            mine = pl.ds(pl.multiple_of((i + 1 + RADIUS) * block, block), block)
            places = [
                jnp.minimum(
                    lax.rem(
                        cube_lists[first_target + t, first + i] - first + BEFORE + total_rows,
                        total_rows,
                    ),
                    2 * BAND_PAIRS - 1,
                )
                for t in range(share)
            ]
            right = jnp.concatenate([square[c, rows, :] for c in places], axis=1)
            cube = jnp.dot(left, right, preferred_element_type=jnp.float32)
            for t, c in enumerate(places):
                own = square[c, mine, :].astype(jnp.float32)
                out_ref[i, t] = 3.0 * own - 2.0 * cube[:, t * block : (t + 1) * block]
        return carry

    lax.fori_loop(0, ROWS // 2, cubes, 0)

    for c in started:
        arrived(c)
        c.wait_send()


N_COPIES = 47
def per_device(density, pattern, square_filter, cube_filter):
    part, block = density.shape[2:]
    share = cube_filter.shape[1] // COLS
    smem = pl.BlockSpec(memory_space=pltpu.SMEM)
    vmem = pl.BlockSpec(memory_space=pltpu.VMEM)

    return pl.pallas_call(
        purify_kernel,
        out_shape=jax.ShapeDtypeStruct((ROWS, share, block, block), jnp.float32),
        in_specs=[smem, smem, smem, vmem],
        out_specs=vmem,
        scratch_shapes=[
            pltpu.VMEM((BAND_PAIRS, 2 * block, WIDTH * block), density.dtype),
            pltpu.VMEM((2 * BAND_PAIRS, 2 * SQUARE_PAIRS * block, block), density.dtype),
            pltpu.VMEM((N_OWN, part, block), density.dtype),
            pltpu.VMEM((COLS, HELD, part, block), density.dtype),
            pltpu.SMEM((2 * SQUARE_PAIRS, 2 * SQUARE_REACH + 3), jnp.int32),
            pltpu.SemaphoreType.DMA((N_COPIES,)),
            pltpu.SemaphoreType.DMA((N_COPIES,)),
        ],
        compiler_params=pltpu.CompilerParams(
            collective_id=0, has_side_effects=True, vmem_limit_bytes=50 << 20
        ),
        name="purify",
    )(pattern.T, square_filter.T, cube_filter.T, density)


def solution(mesh):
    in_specs = (P(("row", "layer"), None, "col", None), P(), P(), P())
    out_specs = P(("row", "layer"), "col", None, None)
    return jax.shard_map(
        per_device, mesh=mesh, in_specs=in_specs, out_specs=out_specs, check_vma=False
    )
```

```python
import functools

import jax
import jax.numpy as jnp
from jax import lax
from jax.experimental import pallas as pl
from jax.experimental.pallas import tpu as pltpu
from jax.sharding import PartitionSpec as P

MESH = pl.DeviceIdType.MESH
RADIUS = 5
HALF = RADIUS + 1
BAND = 2 * RADIUS + 1
SQUARE_REACH = 2 * RADIUS
ROWS = 8
COLS = 4
BEFORE = 16


BAND_PAIRS = 20
SQUARE_PAIRS = 10
WIDTH = BAND + 1


def block_list():
    within = [(i, d) for d in range(HALF) for i in range(ROWS - d)]
    near = [(i, d) for i, d in within if i < 2]
    tail = [(i, d) for i, d in within if i + d >= ROWS - 2]
    lower = [(i, -d) for i in range(RADIUS) for d in range(i + 1, HALF)]
    early = [b for b in within if b not in near and b not in tail]
    upper = [(i, d) for d in range(1, HALF) for i in range(ROWS - d, ROWS)]
    both = [b for b in tail if b in near]
    near = [b for b in near if b not in both]
    tail = [b for b in tail if b not in both]
    return lower + early + near + both + tail + upper


OWN = block_list()
LOWER = slice(0, 15)
WITHIN = slice(15, 48)
EDGE = slice(25, 37)
FAR = slice(36, 63)
N_OWN = len(OWN)
AT_ACROSS = N_OWN
AT_RELAY = AT_ACROSS + 33
AT_FAR = AT_RELAY + 33
AT_LOWER = AT_FAR + 27
AT_EDGE = AT_LOWER + 15
HELD = AT_EDGE + 12


def purify_kernel(
    pattern_hbm,
    square_lists_hbm,
    cube_lists_hbm,
    density_hbm,
    out_ref,
    band_ref,
    square,
    upper,
    held,
    member,
    pattern,
    square_lists,
    cube_lists,
    density_ref,
    load,
    send,
    recv,
):
    row, col, layer = (lax.axis_index(a) for a in ("row", "col", "layer"))
    n_row, n_layer = lax.axis_size("row"), lax.axis_size("layer")
    side = lax.rem(layer, 2)
    up = lax.div(layer + 2, n_layer)
    down = 1 - lax.div(layer + n_layer - 2, n_layer)
    partner = {"layer": layer + 1 - 2 * side}
    after = {"row": lax.rem(row + up, n_row), "layer": lax.rem(layer + 2, n_layer)}
    before = {
        "row": lax.rem(row + n_row - down, n_row),
        "layer": lax.rem(layer + n_layer - 2, n_layer),
    }
    relay = {k: after[k] * (1 - side) + before[k] * side for k in after}
    right, left = lax.rem(col + 1, COLS), lax.rem(col + COLS - 1, COLS)
    block = density_ref.shape[-1]

    barrier = pltpu.get_barrier_semaphore()
    for peer in (partner, after, before, {"col": left}, {"col": right}):
        pl.semaphore_signal(barrier, inc=1, device_id=peer, device_id_type=MESH)

    loads = [
        pltpu.make_async_copy(src, dst, load.at[n])
        for n, (src, dst) in enumerate(
            (
                (pattern_hbm, pattern),
                (density_hbm, density_ref),
                (square_lists_hbm, square_lists),
                (cube_lists_hbm, cube_lists),
            )
        )
    ]
    for one in loads:
        one.start()
    loads[0].wait()
    loads[1].wait()
    slots, total_rows = pattern.shape
    first = (row * n_layer + layer) * ROWS

    def take_own(blocks):
        for n in range(blocks.start, blocks.stop):
            i, d = OWN[n]
            target = lax.rem(first + i + d + total_rows, total_rows)
            slot = jnp.int32(-1)
            for s in range(slots):
                slot = jnp.where(pattern[s, first + i] == target, s, slot)
            found = density_ref[i, jnp.maximum(slot, 0)]
            upper[n] = jnp.where(slot >= 0, found, jnp.zeros_like(found))

    take_own(WITHIN)
    pl.semaphore_wait(barrier, 5)

    started, waited = [], set()

    def copy(src, dst, device, start=True):
        n = len(started)
        c = pltpu.make_async_remote_copy(
            src_ref=src,
            dst_ref=dst,
            send_sem=send.at[n],
            recv_sem=recv.at[n],
            device_id=device,
            device_id_type=MESH,
        )
        if start:
            c.start()
        started.append(c)
        return c

    def arrived(c):
        if id(c) not in waited:
            c.wait_recv()
            waited.add(id(c))

    def spread(src, at, n):
        rows = pl.ds(at, n)
        return (
            copy(src, held.at[col, rows], {"col": right}),
            copy(src, held.at[col, rows], {"col": left}),
        )

    def forward(pair, at, n):
        half = n // 2
        arrived(pair[0])
        a = held.at[left, pl.ds(at, half)]
        first = copy(a, a, {"col": right})
        arrived(pair[1])
        b = held.at[right, pl.ds(at + half, n - half)]
        return first, copy(b, b, {"col": left})

    def sideways(at, n, from_y, start=True):
        rows = pl.ds(at, n)
        a, b = held.at[col, rows], held.at[left, rows]
        pair = copy(a, a, {"col": left}, False), copy(b, b, {"col": right}, False)
        if start:
            go_sideways(pair, from_y)
        return pair

    def go_sideways(pair, from_y):
        for c, source in zip(pair, from_y):
            source.wait_recv()
            waited.add(id(source))
            c.start()

    def place(whole, base, p, d):
        lane = (p % 2 + RADIUS + d) * block
        row = p % 2 * block
        band_ref[base + p // 2, row : row + block, lane : lane + block] = whole

    def unfold(at, blocks, base):
        for n, (i, d) in enumerate(blocks):
            parts = [held[c, at + n] for c in range(COLS)]
            whole = jnp.concatenate(parts, axis=0)
            place(whole, base, i, d)
            if d:
                place(whole.T, base, i + d, -d)

    pieces = 3
    size = 33 // pieces
    seen = 12 - 8 * side
    seen_as = 4 + 8 * side
    own_parts = ((36, 27), (0, 36))
    across = [
        copy(
            upper.at[pl.ds(WITHIN.start + k * size, size)],
            held.at[col, pl.ds(AT_ACROSS + k * size, size)],
            partner,
        )
        for k in range(pieces)
    ]
    take_own(slice(WITHIN.stop, N_OWN))
    take_own(LOWER)
    own_pairs = [spread(upper.at[pl.ds(at, n)], at, n) for at, n in own_parts]
    groups = (
        (FAR, AT_FAR, after),
        (LOWER, AT_LOWER, before),
        (EDGE, AT_EDGE, before),
    )
    first_slices = [
        copy(upper.at[g], held.at[col, pl.ds(at, g.stop - g.start)], device)
        for g, at, device in groups
    ]
    held[col, 0:N_OWN] = upper[...]

    def zero_band():
        for n in range(BAND_PAIRS):
            if 5 <= n < 15:
                corner = jnp.zeros((block, block), band_ref.dtype)
                band_ref[n, 0:block, BAND * block :] = corner
                band_ref[n, block:, 0:block] = corner
            else:
                band_ref[n] = jnp.zeros_like(band_ref[n])

    def zero_square():
        for j in range(BAND_PAIRS):
            for k in range(SQUARE_PAIRS):
                if abs(j - k - 5) > RADIUS:
                    for h in range(2):
                        square[2 * j + h, 2 * k * block : 2 * (k + 1) * block, :] = jnp.zeros(
                            (2 * block, block), square.dtype
                        )

    reach = SQUARE_REACH + 1

    def table(k, carry):
        at = lax.rem(first + k - RADIUS - 1 + total_rows, total_rows)
        listed = [square_lists[s, at] for s in range(square_lists.shape[0])]
        for e in range(2 * reach + 1):
            target = lax.rem(at + e - reach + total_rows, total_rows)
            kept = jnp.int32(0)
            for one in listed:
                kept = jnp.where(one == target, 1, kept)
            member[k, e] = kept
        return carry

    def square_pair(k, j, e, a, b):
        width = (WIDTH - 2 * abs(e)) * block
        turned = (j - k) * 2 + reach
        value = lax.dot_general(
            band_ref[k, :, pl.ds(pl.multiple_of(a, block), width)],
            band_ref[j, :, pl.ds(pl.multiple_of(b, block), width)],
            (((1,), (1,)), ((), ())),
            preferred_element_type=jnp.float32,
        )
        for hj in range(2):
            for hk in range(2):
                at = 2 * (k - 5) + hk
                kept = member[at, turned + hj - hk] == 1
                part = value[hk * block : (hk + 1) * block, hj * block : (hj + 1) * block]
                rows = pl.ds(pl.multiple_of(at * block, block), block)
                square[2 * j + hj, rows, :] = jnp.where(kept, part, 0.0).astype(square.dtype)

    def straight(k, e):
        square_pair(k, k + e, e, max(2 * e, 0) * block, max(-2 * e, 0) * block)

    def square_rows(k, carry):
        for e in range(-RADIUS, RADIUS + 1):
            straight(k, e)
        return carry

    def mirrored(k, j):
        e = j - k
        a, b = max(2 * e, 0) * block, max(-2 * e, 0) * block
        square_pair(
            k + side * (19 - 2 * k), j + side * (19 - 2 * j), e, a + side * (b - a), b + side * (a - b)
        )

    zero_band()
    loads[2].wait()
    loads[3].wait()
    arrived(own_pairs[0][0])

    def second(n):
        g, at, device = groups[n]
        return copy(held.at[left, g], held.at[left, pl.ds(at, g.stop - g.start)], device)

    second_slices = [second(0)]
    lax.fori_loop(0, 2 * SQUARE_PAIRS, table, 0)
    arrived(own_pairs[1][0])
    second_slices += [second(1), second(2)]
    own_last = [forward(p, at, n) for p, (at, n) in zip(own_pairs, own_parts)]
    side_last = [
        sideways(at, g.stop - g.start, None, False) for g, at, _ in groups
    ]
    far_late = (layer < 2) & (lax.rem(row, 2) == 0)
    near_late = (layer >= n_layer - 2) & (lax.rem(row, 2) == 1)
    late = (far_late, near_late, near_late)
    bases = (0, BEFORE // 2 + ROWS, BEFORE // 2 + ROWS)

    def take_side(n):
        go_sideways(side_last[n], (first_slices[n], second_slices[n]))

    def unfold_side(n):
        g, at, _ = groups[n]
        for c in side_last[n]:
            c.wait_recv()
            waited.add(id(c))
        unfold(at, OWN[g], bases[n])

    for n in range(3):
        pl.when(jnp.logical_not(late[n]))(functools.partial(take_side, n))
    zero_square()

    across_pairs, relay_first, relay_second, across_last, relay_last = [], [], [], [], []

    def take_across(k):
        arrived(across[k])
        at, put = AT_ACROSS + k * size, AT_RELAY + k * size
        src = held.at[col, pl.ds(at, size)]
        relay_first.append(copy(src, held.at[col, pl.ds(put, size)], relay))
        across_pairs.append(spread(src, at, size))

    def pass_on(k):
        at, put = AT_ACROSS + k * size, AT_RELAY + k * size
        arrived(across_pairs[k][0])
        src = held.at[left, pl.ds(at, size)]
        relay_second.append(copy(src, held.at[left, pl.ds(put, size)], relay))
        across_last.append(forward(across_pairs[k], at, size))

    def unfold_piece(at0, k, last, base):
        for c in last:
            arrived(c)
        at = WITHIN.start + k * size
        unfold(at0 + k * size, OWN[at : at + size], base)

    take_across(0)
    for n in range(2):
        at, count = own_parts[n]
        for c in own_last[n]:
            arrived(c)
        unfold(at, OWN[at : at + count], BEFORE // 2)
    take_across(1)
    pass_on(0)
    for n in range(3):
        pl.when(late[n])(functools.partial(take_side, n))

    for k in range(8, 12):
        for j in range(8, 12):
            straight(k, j - k)

    for n in range(3):
        pl.when(jnp.logical_not(late[n]))(functools.partial(unfold_side, n))
    take_across(2)
    pass_on(1)
    pass_on(2)
    for n in range(3):
        pl.when(late[n])(functools.partial(unfold_side, n))
    for k in range(pieces):
        at = AT_RELAY + k * size
        relay_last.append(sideways(at, size, (relay_first[k], relay_second[k])))
    for k in range(pieces):
        unfold_piece(AT_ACROSS, k, across_last[k], seen)

    lax.fori_loop(12 - 7 * side, 15 - 7 * side, square_rows, 0)
    for k in range(8, 12):
        for j in range(k - RADIUS, k + RADIUS + 1):
            if not 4 <= j < 12:
                mirrored(k, j)
    for k in range(pieces):
        unfold_piece(AT_RELAY, k, relay_last[k], seen_as)
    lax.fori_loop(5 + 7 * side, 8 + 7 * side, square_rows, 0)
    for k in range(8, 13):
        for j in range(max(4, k - RADIUS), 8):
            mirrored(k, j)

    share = out_ref.shape[1]
    first_target = col * share

    def cubes(n, carry):
        for h in range(2):
            i = 2 * n + h
            left = band_ref[n + BEFORE // 2, h * block : (h + 1) * block, h * block : (h + BAND) * block]
            rows = pl.ds(pl.multiple_of((i + 1) * block, block), BAND * block)
            mine = pl.ds(pl.multiple_of((i + 1 + RADIUS) * block, block), block)
            places = [
                jnp.minimum(
                    lax.rem(
                        cube_lists[first_target + t, first + i] - first + BEFORE + total_rows,
                        total_rows,
                    ),
                    2 * BAND_PAIRS - 1,
                )
                for t in range(share)
            ]
            right = jnp.concatenate([square[c, rows, :] for c in places], axis=1)
            cube = jnp.dot(left, right, preferred_element_type=jnp.float32)
            for t, c in enumerate(places):
                own = square[c, mine, :].astype(jnp.float32)
                out_ref[i, t] = 3.0 * own - 2.0 * cube[:, t * block : (t + 1) * block]
        return carry

    lax.fori_loop(0, ROWS // 2, cubes, 0)

    for c in started:
        arrived(c)
        c.wait_send()


N_COPIES = 47
def per_device(density, pattern, square_filter, cube_filter):
    part, block = density.shape[2:]
    share = cube_filter.shape[1] // COLS
    hbm = pl.BlockSpec(memory_space=pltpu.HBM)
    vmem = pl.BlockSpec(memory_space=pltpu.VMEM)

    return pl.pallas_call(
        purify_kernel,
        out_shape=jax.ShapeDtypeStruct((ROWS, share, block, block), jnp.float32),
        in_specs=[hbm] * 4,
        out_specs=vmem,
        scratch_shapes=[
            pltpu.VMEM((BAND_PAIRS, 2 * block, WIDTH * block), density.dtype),
            pltpu.VMEM((2 * BAND_PAIRS, 2 * SQUARE_PAIRS * block, block), density.dtype),
            pltpu.VMEM((N_OWN, part, block), density.dtype),
            pltpu.VMEM((COLS, HELD, part, block), density.dtype),
            pltpu.SMEM((2 * SQUARE_PAIRS, 2 * SQUARE_REACH + 3), jnp.int32),
            pltpu.SMEM(pattern.shape[::-1], jnp.int32),
            pltpu.SMEM(square_filter.shape[::-1], jnp.int32),
            pltpu.SMEM(cube_filter.shape[::-1], jnp.int32),
            pltpu.VMEM((ROWS, *density.shape[1:]), density.dtype),
            pltpu.SemaphoreType.DMA((4,)),
            pltpu.SemaphoreType.DMA((N_COPIES,)),
            pltpu.SemaphoreType.DMA((N_COPIES,)),
        ],
        compiler_params=pltpu.CompilerParams(
            collective_id=0, has_side_effects=True, vmem_limit_bytes=60 << 20
        ),
        name="purify",
    )(pattern.T, square_filter.T, cube_filter.T, density)


def solution(mesh):
    in_specs = (P(("row", "layer"), None, "col", None), P(), P(), P())
    out_specs = P(("row", "layer"), "col", None, None)
    return jax.shard_map(
        per_device, mesh=mesh, in_specs=in_specs, out_specs=out_specs, check_vma=False
    )
```

```python
import functools

import jax
import jax.numpy as jnp
from jax import lax
from jax.experimental import pallas as pl
from jax.experimental.pallas import tpu as pltpu
from jax.sharding import PartitionSpec as P

MESH = pl.DeviceIdType.MESH
RADIUS = 5
HALF = RADIUS + 1
BAND = 2 * RADIUS + 1
SQUARE_REACH = 2 * RADIUS
ROWS = 8
COLS = 4
BEFORE = 16


BAND_PAIRS = 20
SQUARE_PAIRS = 10
WIDTH = BAND + 1


def block_list():
    within = [(i, d) for d in range(HALF) for i in range(ROWS - d)]
    near = [(i, d) for i, d in within if i < 2]
    tail = [(i, d) for i, d in within if i + d >= ROWS - 2]
    lower = [(i, -d) for i in range(RADIUS) for d in range(i + 1, HALF)]
    early = [b for b in within if b not in near and b not in tail]
    upper = [(i, d) for d in range(1, HALF) for i in range(ROWS - d, ROWS)]
    both = [b for b in tail if b in near]
    near = [b for b in near if b not in both]
    tail = [b for b in tail if b not in both]
    return lower + early + near + both + tail + upper


OWN = block_list()
LOWER = slice(0, 15)
WITHIN = slice(15, 48)
EDGE = slice(25, 37)
FAR = slice(36, 63)
N_OWN = len(OWN)
AT_ACROSS = N_OWN
AT_RELAY = AT_ACROSS + 33
AT_FAR = AT_RELAY + 33
AT_LOWER = AT_FAR + 27
AT_EDGE = AT_LOWER + 15
HELD = AT_EDGE + 12


def purify_kernel(
    pattern_hbm,
    square_lists_hbm,
    cube_lists_hbm,
    density_hbm,
    out_ref,
    band_ref,
    square,
    upper,
    held,
    member,
    pattern,
    square_lists,
    cube_lists,
    density_ref,
    load,
    send,
    recv,
):
    row, col, layer = (lax.axis_index(a) for a in ("row", "col", "layer"))
    n_row, n_layer = lax.axis_size("row"), lax.axis_size("layer")
    side = lax.rem(layer, 2)
    up = lax.div(layer + 2, n_layer)
    down = 1 - lax.div(layer + n_layer - 2, n_layer)
    partner = {"layer": layer + 1 - 2 * side}
    after = {"row": lax.rem(row + up, n_row), "layer": lax.rem(layer + 2, n_layer)}
    before = {
        "row": lax.rem(row + n_row - down, n_row),
        "layer": lax.rem(layer + n_layer - 2, n_layer),
    }
    relay = {k: after[k] * (1 - side) + before[k] * side for k in after}
    right, left = lax.rem(col + 1, COLS), lax.rem(col + COLS - 1, COLS)
    block = density_ref.shape[-1]

    barrier = pltpu.get_barrier_semaphore()
    for peer in (partner, after, before, {"col": left}, {"col": right}):
        pl.semaphore_signal(barrier, inc=1, device_id=peer, device_id_type=MESH)

    loads = [
        pltpu.make_async_copy(src, dst, load.at[n])
        for n, (src, dst) in enumerate(
            (
                (pattern_hbm, pattern),
                (density_hbm, density_ref),
                (square_lists_hbm, square_lists),
                (cube_lists_hbm, cube_lists),
            )
        )
    ]
    for one in loads:
        one.start()
    loads[0].wait()
    loads[1].wait()
    slots, total_rows = pattern.shape
    first = (row * n_layer + layer) * ROWS

    def take_own(blocks):
        for n in range(blocks.start, blocks.stop):
            i, d = OWN[n]
            target = lax.rem(first + i + d + total_rows, total_rows)
            slot = jnp.int32(-1)
            for s in range(slots):
                slot = jnp.where(pattern[s, first + i] == target, s, slot)
            found = density_ref[i, jnp.maximum(slot, 0)]
            upper[n] = jnp.where(slot >= 0, found, jnp.zeros_like(found))

    take_own(WITHIN)
    pl.semaphore_wait(barrier, 5)

    started, waited = [], set()

    def copy(src, dst, device, start=True):
        n = len(started)
        c = pltpu.make_async_remote_copy(
            src_ref=src,
            dst_ref=dst,
            send_sem=send.at[n],
            recv_sem=recv.at[n],
            device_id=device,
            device_id_type=MESH,
        )
        if start:
            c.start()
        started.append(c)
        return c

    def arrived(c):
        if id(c) not in waited:
            c.wait_recv()
            waited.add(id(c))

    def spread(src, at, n):
        rows = pl.ds(at, n)
        return (
            copy(src, held.at[col, rows], {"col": right}),
            copy(src, held.at[col, rows], {"col": left}),
        )

    def forward(pair, at, n):
        half = n // 2
        arrived(pair[0])
        a = held.at[left, pl.ds(at, half)]
        first = copy(a, a, {"col": right})
        arrived(pair[1])
        b = held.at[right, pl.ds(at + half, n - half)]
        return first, copy(b, b, {"col": left})

    def sideways(at, n, from_y, start=True):
        rows = pl.ds(at, n)
        a, b = held.at[col, rows], held.at[left, rows]
        pair = copy(a, a, {"col": left}, False), copy(b, b, {"col": right}, False)
        if start:
            go_sideways(pair, from_y)
        return pair

    def go_sideways(pair, from_y):
        for c, source in zip(pair, from_y):
            source.wait_recv()
            waited.add(id(source))
            c.start()

    def place(whole, base, p, d):
        lane = (p % 2 + RADIUS + d) * block
        row = p % 2 * block
        band_ref[base + p // 2, row : row + block, lane : lane + block] = whole

    def unfold(at, blocks, base):
        for n, (i, d) in enumerate(blocks):
            parts = [held[c, at + n] for c in range(COLS)]
            whole = jnp.concatenate(parts, axis=0)
            place(whole, base, i, d)
            if d:
                place(whole.T, base, i + d, -d)

    pieces = 3
    size = 33 // pieces
    seen = 12 - 8 * side
    seen_as = 4 + 8 * side
    own_parts = ((36, 27), (0, 36))
    across = [
        copy(
            upper.at[pl.ds(WITHIN.start + k * size, size)],
            held.at[col, pl.ds(AT_ACROSS + k * size, size)],
            partner,
        )
        for k in range(pieces)
    ]
    take_own(slice(WITHIN.stop, N_OWN))
    take_own(LOWER)
    own_pairs = [spread(upper.at[pl.ds(at, n)], at, n) for at, n in own_parts]
    groups = (
        (FAR, AT_FAR, after),
        (LOWER, AT_LOWER, before),
        (EDGE, AT_EDGE, before),
    )
    first_slices = [
        copy(upper.at[g], held.at[col, pl.ds(at, g.stop - g.start)], device)
        for g, at, device in groups
    ]
    held[col, 0:N_OWN] = upper[...]

    def zero_band():
        for n in range(BAND_PAIRS):
            if 5 <= n < 15:
                corner = jnp.zeros((block, block), band_ref.dtype)
                band_ref[n, 0:block, BAND * block :] = corner
                band_ref[n, block:, 0:block] = corner
            else:
                band_ref[n] = jnp.zeros_like(band_ref[n])

    def zero_square():
        for j in range(BAND_PAIRS):
            for k in range(SQUARE_PAIRS):
                if abs(j - k - 5) > RADIUS:
                    for h in range(2):
                        square[2 * j + h, 2 * k * block : 2 * (k + 1) * block, :] = jnp.zeros(
                            (2 * block, block), square.dtype
                        )

    reach = SQUARE_REACH + 1

    def table(k, carry):
        at = lax.rem(first + k - RADIUS - 1 + total_rows, total_rows)
        listed = [square_lists[s, at] for s in range(square_lists.shape[0])]
        for e in range(2 * reach + 1):
            target = lax.rem(at + e - reach + total_rows, total_rows)
            kept = jnp.int32(0)
            for one in listed:
                kept = jnp.where(one == target, 1, kept)
            member[k, e] = kept
        return carry

    def square_pair(k, j, e, a, b):
        width = (WIDTH - 2 * abs(e)) * block
        turned = (j - k) * 2 + reach
        value = lax.dot_general(
            band_ref[k, :, pl.ds(pl.multiple_of(a, block), width)],
            band_ref[j, :, pl.ds(pl.multiple_of(b, block), width)],
            (((1,), (1,)), ((), ())),
            preferred_element_type=jnp.float32,
        )
        for hj in range(2):
            for hk in range(2):
                at = 2 * (k - 5) + hk
                kept = member[at, turned + hj - hk] == 1
                part = value[hk * block : (hk + 1) * block, hj * block : (hj + 1) * block]
                rows = pl.ds(pl.multiple_of(at * block, block), block)
                square[2 * j + hj, rows, :] = jnp.where(kept, part, 0.0).astype(square.dtype)

    def straight(k, e):
        square_pair(k, k + e, e, max(2 * e, 0) * block, max(-2 * e, 0) * block)

    def square_rows(k, carry):
        for e in range(-RADIUS, RADIUS + 1):
            straight(k, e)
        return carry

    def mirrored(k, j):
        e = j - k
        a, b = max(2 * e, 0) * block, max(-2 * e, 0) * block
        square_pair(
            k + side * (19 - 2 * k), j + side * (19 - 2 * j), e, a + side * (b - a), b + side * (a - b)
        )

    zero_band()
    loads[2].wait()
    loads[3].wait()
    arrived(own_pairs[0][0])

    def second(n):
        g, at, device = groups[n]
        return copy(held.at[left, g], held.at[left, pl.ds(at, g.stop - g.start)], device)

    second_slices = [second(0)]
    lax.fori_loop(0, 2 * SQUARE_PAIRS, table, 0)
    arrived(own_pairs[1][0])
    second_slices += [second(1), second(2)]
    own_last = [forward(p, at, n) for p, (at, n) in zip(own_pairs, own_parts)]
    side_last = [
        sideways(at, g.stop - g.start, None, False) for g, at, _ in groups
    ]
    far_late = (layer < 2) & (lax.rem(row, 2) == 0)
    near_late = (layer >= n_layer - 2) & (lax.rem(row, 2) == 1)
    late = (far_late, near_late, near_late)
    bases = (0, BEFORE // 2 + ROWS, BEFORE // 2 + ROWS)

    def take_side(n):
        go_sideways(side_last[n], (first_slices[n], second_slices[n]))

    def unfold_side(n):
        g, at, _ = groups[n]
        for c in side_last[n]:
            c.wait_recv()
            waited.add(id(c))
        unfold(at, OWN[g], bases[n])

    for n in range(3):
        pl.when(jnp.logical_not(late[n]))(functools.partial(take_side, n))
    zero_square()

    across_pairs, relay_first, relay_second, across_last, relay_last = [], [], [], [], []

    def take_across(k):
        arrived(across[k])
        at, put = AT_ACROSS + k * size, AT_RELAY + k * size
        src = held.at[col, pl.ds(at, size)]
        relay_first.append(copy(src, held.at[col, pl.ds(put, size)], relay))
        across_pairs.append(spread(src, at, size))

    def pass_on(k):
        at, put = AT_ACROSS + k * size, AT_RELAY + k * size
        arrived(across_pairs[k][0])
        src = held.at[left, pl.ds(at, size)]
        relay_second.append(copy(src, held.at[left, pl.ds(put, size)], relay))
        across_last.append(forward(across_pairs[k], at, size))

    def unfold_piece(at0, k, last, base):
        for c in last:
            arrived(c)
        at = WITHIN.start + k * size
        unfold(at0 + k * size, OWN[at : at + size], base)

    take_across(0)
    for n in range(2):
        at, count = own_parts[n]
        for c in own_last[n]:
            arrived(c)
        unfold(at, OWN[at : at + count], BEFORE // 2)
    take_across(1)
    pass_on(0)
    for n in range(3):
        pl.when(late[n])(functools.partial(take_side, n))

    for k in range(8, 12):
        for j in range(8, 12):
            straight(k, j - k)

    for n in range(3):
        pl.when(jnp.logical_not(late[n]))(functools.partial(unfold_side, n))
    take_across(2)
    pass_on(1)
    pass_on(2)
    for n in range(3):
        pl.when(late[n])(functools.partial(unfold_side, n))
    for k in range(pieces):
        if k == pieces - 1:
            unfold_piece(AT_ACROSS, k, across_last[k], seen)
        at = AT_RELAY + k * size
        relay_last.append(sideways(at, size, (relay_first[k], relay_second[k])))
        if k < pieces - 1:
            unfold_piece(AT_ACROSS, k, across_last[k], seen)

    lax.fori_loop(12 - 7 * side, 15 - 7 * side, square_rows, 0)
    for k in range(8, 12):
        for j in range(k - RADIUS, k + RADIUS + 1):
            if not 4 <= j < 12:
                mirrored(k, j)
    for k in range(pieces):
        unfold_piece(AT_RELAY, k, relay_last[k], seen_as)
    lax.fori_loop(5 + 7 * side, 8 + 7 * side, square_rows, 0)
    for k in range(8, 13):
        for j in range(max(4, k - RADIUS), 8):
            mirrored(k, j)

    share = out_ref.shape[1]
    first_target = col * share

    def cubes(n, carry):
        for h in range(2):
            i = 2 * n + h
            left = band_ref[n + BEFORE // 2, h * block : (h + 1) * block, h * block : (h + BAND) * block]
            rows = pl.ds(pl.multiple_of((i + 1) * block, block), BAND * block)
            mine = pl.ds(pl.multiple_of((i + 1 + RADIUS) * block, block), block)
            places = [
                jnp.minimum(
                    lax.rem(
                        cube_lists[first_target + t, first + i] - first + BEFORE + total_rows,
                        total_rows,
                    ),
                    2 * BAND_PAIRS - 1,
                )
                for t in range(share)
            ]
            right = jnp.concatenate([square[c, rows, :] for c in places], axis=1)
            cube = jnp.dot(left, right, preferred_element_type=jnp.float32)
            for t, c in enumerate(places):
                own = square[c, mine, :].astype(jnp.float32)
                out_ref[i, t] = 3.0 * own - 2.0 * cube[:, t * block : (t + 1) * block]
        return carry

    lax.fori_loop(0, ROWS // 2, cubes, 0)

    for c in started:
        arrived(c)
        c.wait_send()


N_COPIES = 47
def per_device(density, pattern, square_filter, cube_filter):
    part, block = density.shape[2:]
    share = cube_filter.shape[1] // COLS
    hbm = pl.BlockSpec(memory_space=pltpu.HBM)
    vmem = pl.BlockSpec(memory_space=pltpu.VMEM)

    return pl.pallas_call(
        purify_kernel,
        out_shape=jax.ShapeDtypeStruct((ROWS, share, block, block), jnp.float32),
        in_specs=[hbm] * 4,
        out_specs=vmem,
        scratch_shapes=[
            pltpu.VMEM((BAND_PAIRS, 2 * block, WIDTH * block), density.dtype),
            pltpu.VMEM((2 * BAND_PAIRS, 2 * SQUARE_PAIRS * block, block), density.dtype),
            pltpu.VMEM((N_OWN, part, block), density.dtype),
            pltpu.VMEM((COLS, HELD, part, block), density.dtype),
            pltpu.SMEM((2 * SQUARE_PAIRS, 2 * SQUARE_REACH + 3), jnp.int32),
            pltpu.SMEM(pattern.shape[::-1], jnp.int32),
            pltpu.SMEM(square_filter.shape[::-1], jnp.int32),
            pltpu.SMEM(cube_filter.shape[::-1], jnp.int32),
            pltpu.VMEM((ROWS, *density.shape[1:]), density.dtype),
            pltpu.SemaphoreType.DMA((4,)),
            pltpu.SemaphoreType.DMA((N_COPIES,)),
            pltpu.SemaphoreType.DMA((N_COPIES,)),
        ],
        compiler_params=pltpu.CompilerParams(
            collective_id=0, has_side_effects=True, vmem_limit_bytes=60 << 20
        ),
        name="purify",
    )(pattern.T, square_filter.T, cube_filter.T, density)


def solution(mesh):
    in_specs = (P(("row", "layer"), None, "col", None), P(), P(), P())
    out_specs = P(("row", "layer"), "col", None, None)
    return jax.shard_map(
        per_device, mesh=mesh, in_specs=in_specs, out_specs=out_specs, check_vma=False
    )
```
